512 devices in a mesh: dp: 8 (over z_hi, core), expert: 16 (over x, y), tensor: 4 (over z_lo).
Axes of the slice: x: 4, y: 4, z: 16 (z_hi: 4, z_lo: 4; z = z_hi * 4 + z_lo), core: 2. Of those that a mesh axis runs over, the one named last changes fastest.
Arguments:
- hidden_in: bfloat16 [16384, 2048], P(('dp', 'expert'), 'tensor'), may hold values from -6 to 6
- queries: bfloat16 [16384, 2048], P(('dp', 'expert'), 'tensor'), may hold values from -6 to 6
- new_keys: bfloat16 [16384, 2048], P(('dp', 'expert'), 'tensor'), may hold values from -6 to 6
- new_values: bfloat16 [16384, 2048], P(('dp', 'expert'), 'tensor'), may hold values from -6 to 6
- prefix_keys: bfloat16 [2048, 2048], P('dp', 'tensor'), may hold values from -6 to 6
- prefix_values: bfloat16 [2048, 2048], P('dp', 'tensor'), may hold values from -6 to 6
- node_length: int32 [32], replicated, may hold values from 1 to 64, as said below
- parent: int32 [32], replicated, may hold values from 0 to 31, as said below
- leaf_of_request: int32 [256], P(('dp', 'expert')), may hold values from 0 to 30, as said below
- out_weight: bfloat16 [2048, 2048], P('tensor', 'expert'), may hold values from -0.125 to 0.125
- norm_gain: float32 [2048], P('tensor'), may hold values from 0.25 to 1.75
- expert_ids: int32 [16384, 8], P(('dp', 'expert')), may hold values from 0 to 15, all different within a row; in each aligned block of 128 rows (0 to 127, 128 to 255, ...) at most 72 rows name the same one
- gate_weights: float32 [16384, 8], P(('dp', 'expert')), may hold values from 0.05 to 0.5
- gate_up: bfloat16 [16, 2, 2048, 1024], P('expert', None, None, 'tensor'), may hold values from -0.125 to 0.125
- down_weight: bfloat16 [16, 1024, 2048], P('expert', 'tensor'), may hold values from -0.1875 to 0.1875
Outputs:
- layer_out: bfloat16 [16384, 2048], P(('dp', 'expert'), 'tensor')
The draws below stay inside these ranges and needn't reach their ends.
Inputs may be any that keep to these rules, and one draw needn't show every extreme that they name: `node_length`: the root node holds 64 live rows and some leaf a single one. One root node is its own parent; four tenant nodes have the root as parent; every other node is a leaf whose parent is a tenant node. `leaf_of_request`: every request names a leaf node. `expert_ids`: each row names 8 different experts; among the 128 rows of one device no expert is named more than 72 times.
All inputs are finite; a program needn't handle non-finite values.
Results may differ from the reference program's by a relative error of at most 0.014.
Values may be sent and summed in bfloat16 or wider, within the bound.
A program may use at most 64 MiB of HBM per device.

```python
import math
import jax
import jax.numpy as jnp
import numpy as np
from jax import lax

D = 2048
HEADS = 16
HEAD_DIM = 128
FF = 1024
REQ_LEN = 64
NODE_LEN = 64
TOK_DEV = 128
CAP = 72
TOPK = 8
EXPERTS = 16
NODES = 32
REQUESTS = 256
TOKENS = 16384
N_TENSOR = 4


def node_order(key):
    shuffled = jax.random.permutation(jax.random.fold_in(key, 101), NODES - 2).astype(jnp.int32)
    head = jnp.array([NODES - 1], jnp.int32)
    tail = jnp.array([NODES - 2], jnp.int32)
    return jnp.concatenate([head, shuffled, tail]).astype(jnp.int32)


def tenant_of_leaf(key):
    leaf_count = NODES - 5
    picks = jax.random.randint(jax.random.fold_in(key, 102), (leaf_count,), 0, 10)
    tenant_table = jnp.array([0, 0, 0, 0, 1, 1, 1, 2, 2, 3], jnp.int32)
    skewed = jnp.sum(jnp.where(picks[:, None] == jnp.arange(10, dtype=jnp.int32)[None, :], tenant_table[None, :], 0), axis=1)
    leaf_rank = jnp.arange(leaf_count, dtype=jnp.int32)
    return jnp.where(leaf_rank < 4, leaf_rank, skewed).astype(jnp.int32)


def draw_parent(key, part):
    ordering = node_order(key)
    root_node = ordering[0]
    result = jnp.zeros((NODES,), jnp.int32)
    result = result.at[root_node].set(root_node)
    result = result.at[ordering[1:5]].set(root_node)
    result = result.at[ordering[5:]].set(ordering[1 + tenant_of_leaf(key)])
    return result


def draw_node_length(key, part):
    ordering = node_order(key)
    length = jax.random.randint(jax.random.fold_in(key, 103), (NODES,), 1, NODE_LEN + 1).astype(jnp.int32)
    length = length.at[ordering[0]].set(NODE_LEN)
    length = length.at[ordering[NODES - 1]].set(1)
    return length


def draw_leaf_of_request(key, part):
    ordering = node_order(key)
    leaf_count = NODES - 5
    first_pick = jax.random.randint(jax.random.fold_in(key, 104), (REQUESTS,), 0, leaf_count)
    second_pick = jax.random.randint(jax.random.fold_in(key, 105), (REQUESTS,), 0, leaf_count)
    chosen = jnp.minimum(first_pick, second_pick)
    request_index = jnp.arange(REQUESTS, dtype=jnp.int32)
    chosen = jnp.where(request_index == 0, leaf_count - 1, chosen)
    return ordering[5 + chosen].astype(jnp.int32)


def draw_queries(key, part):
    base_key = jax.random.fold_in(key, 201)
    array_shape = (TOKENS, HEADS * HEAD_DIM)
    values = jnp.clip(jax.random.normal(base_key, array_shape, jnp.float32), -6.0, 6.0)
    return values.astype(jnp.bfloat16)


def draw_prefix_keys(key, part):
    base_key = jax.random.fold_in(key, 203)
    array_shape = (NODES * NODE_LEN, HEADS * HEAD_DIM)
    values = jnp.clip(jax.random.normal(base_key, array_shape, jnp.float32), -6.0, 6.0)
    return values.astype(jnp.bfloat16)


def block_levels(rng, shape, cuts, least, largest):
    loudness = 1.0
    for dim, shards_of in cuts:
        draws = jax.random.uniform(jax.random.fold_in(jax.random.fold_in(rng, 6), dim), (shards_of,), jnp.float32, least / len(cuts), largest / len(cuts))
        loudness = loudness * jnp.repeat(jnp.exp(draws), shape[dim] // shards_of).reshape((-1,) + (1,) * (len(shape) - 1 - dim))
    return loudness


def shared_out(key, own, number, rows, number_of, top, limit, lean):
    sequence = jax.random.permutation(key, number_of)
    heavy_load, usual = portions_of(number_of, rows * top, limit, lean, True), portions_of(number_of, rows * top, limit, lean, False)
    places = jnp.arange(number_of)

    def named(sizes, turn):
        used = int((sizes > 0).sum())
        fixed = max(1, used // 4)
        passed = fixed + (places - fixed + turn * (used - fixed)) % max(1, number_of - fixed)
        return jnp.zeros((number_of,), jnp.int32).at[sequence[jnp.where(places < fixed, places, passed)]].set(jnp.asarray(sizes, jnp.int32))

    sizes = jnp.where(number % 4 == 0, named(heavy_load, number // 4), named(usual, number - number // 4 - 1))
    mixed = jax.random.permutation(jax.random.fold_in(own, 3), number_of)
    donor, taker = mixed[0:number_of // 2 * 2:2], mixed[1:number_of // 2 * 2:2]
    room = jnp.minimum(sizes[donor] - 1, limit - sizes[taker]) // 2
    room = jnp.where((donor == sequence[0]) | (taker == sequence[0]) | (sizes[taker] == 0), 0, jnp.maximum(room, 0))
    passed = jax.random.randint(jax.random.fold_in(own, 4), (number_of // 2,), 0, 1 << 20) % (room + 1)
    sizes = sizes.at[donor].add(-passed).at[taker].add(passed)
    items = jnp.searchsorted(jnp.cumsum(sizes), jnp.arange(rows * top), side="right").astype(jnp.int32)
    grid = items.reshape(top, rows).T
    grid = grid[jax.random.permutation(jax.random.fold_in(own, 1), rows)]
    turn = jax.random.randint(jax.random.fold_in(own, 2), (rows, 1), 0, top)
    return jnp.take_along_axis(grid, (jnp.arange(top)[None, :] + turn) % top, axis=1)


def portions_of(amount, total, reach, lean, full):
    loads = [(1 << 20) // math.isqrt(standing ** lean) + 1 for standing in range(1, amount + 1)]
    largest = reach if full else min(reach, max(-(-total // amount), total * loads[0] // sum(loads)))
    least = 1 if total - largest >= amount - 1 else 0
    counts, spare = [largest] + [least] * (amount - 1), total - largest - least * (amount - 1)
    while spare > 0:
        free = [i for i in range(1, amount) if counts[i] < largest] or [i for i in range(1, amount) if counts[i] < reach]
        pool, left = sum([loads[i] for i in free]), spare
        for i in free:
            more = min(reach - counts[i], max(1, left * loads[i] // pool), spare)
            counts[i] = counts[i] + more
            spare = spare - more
    return np.array(counts)


def bell_draw(own_key, extent, scale, reach, pieces=(), kind=jnp.bfloat16):
    loudness = block_levels(own_key, extent, pieces, -0.22, 0.18) if pieces else 1.0
    entries = jax.random.normal(own_key, extent, jnp.float32) * scale * loudness
    return jnp.minimum(jnp.maximum(entries, -reach), reach).astype(kind)


def setup_inputs(seed: int = 0) -> dict:
    seeds = jax.random.split(jax.random.key(seed), 16)
    hidden_in = bell_draw(seeds[0], (TOKENS, D), 1.0, 6.0, ((0, 128), (1, 4)))
    queries = draw_queries(jax.random.fold_in(seeds[15], 71), 0)
    new_keys = bell_draw(seeds[2], (TOKENS, HEADS * HEAD_DIM), 1.0, 6.0, ((0, 128), (1, 4)))
    new_values = bell_draw(seeds[3], (TOKENS, HEADS * HEAD_DIM), 1.0, 6.0, ((0, 128), (1, 4)))
    prefix_keys = draw_prefix_keys(jax.random.fold_in(seeds[15], 71), 0)
    prefix_values = bell_draw(seeds[5], (NODES * NODE_LEN, HEADS * HEAD_DIM), 1.0, 6.0, ((0, 8), (1, 4)))
    node_length = draw_node_length(jax.random.fold_in(seeds[15], 71), 0)
    parent = draw_parent(jax.random.fold_in(seeds[15], 71), 0)
    leaf_of_request = draw_leaf_of_request(jax.random.fold_in(seeds[15], 71), 0)
    out_weight = bell_draw(seeds[9], (HEADS * HEAD_DIM, D), (HEADS * HEAD_DIM) ** -0.5, 0.125, ((0, 4), (1, 16)))
    norm_gain = jnp.clip(1.0 + 0.15 * jax.random.normal(seeds[10], (D,), jnp.float32), 0.25, 1.75)
    expert_ids_keys = jax.random.split(jax.random.fold_in(seeds[11], 1), TOKENS // TOK_DEV)
    expert_ids_turns = jax.random.permutation(jax.random.fold_in(seeds[11], 3), TOKENS // TOK_DEV)
    expert_ids = jax.vmap(lambda own, number: shared_out(jax.random.fold_in(seeds[11], 2), own, number, TOK_DEV, EXPERTS, TOPK, CAP, 2))(expert_ids_keys, expert_ids_turns).reshape((TOKENS, TOPK))
    gate_weights = jnp.clip(jnp.exp(math.log(0.5) - 2.3025851 * jax.random.uniform(seeds[12], (TOKENS, TOPK), jnp.float32) ** block_levels(seeds[12], (TOKENS, TOPK), ((0, 128),), -0.2, 0.2)), 0.05, 0.5)
    gate_up = bell_draw(seeds[13], (EXPERTS, 2, D, FF), D ** -0.5, 0.125, ((0, 16), (3, 4)))
    down_weight = bell_draw(seeds[14], (EXPERTS, FF, D), FF ** -0.5, 0.1875, ((0, 16), (1, 4)))
    return dict(hidden_in=hidden_in, queries=queries, new_keys=new_keys, new_values=new_values, prefix_keys=prefix_keys, prefix_values=prefix_values, node_length=node_length, parent=parent, leaf_of_request=leaf_of_request, out_weight=out_weight, norm_gain=norm_gain, expert_ids=expert_ids, gate_weights=gate_weights, gate_up=gate_up, down_weight=down_weight)


floor_score = -1e+30
epsilon = 1e-05

def reference(hidden_in, queries, new_keys, new_values, prefix_keys, prefix_values, node_length, parent, leaf_of_request, out_weight, norm_gain, expert_ids, gate_weights, gate_up, down_weight):
    score_scale = 1.0 / HEAD_DIM ** 0.5
    prefix_key_nodes = prefix_keys.reshape(NODES, NODE_LEN, HEADS, HEAD_DIM)
    prefix_value_nodes = prefix_values.reshape(NODES, NODE_LEN, HEADS, HEAD_DIM)
    query_req = queries.reshape(REQUESTS, REQ_LEN, HEADS, HEAD_DIM)
    key_req = new_keys.reshape(REQUESTS, REQ_LEN, HEADS, HEAD_DIM)
    value_req = new_values.reshape(REQUESTS, REQ_LEN, HEADS, HEAD_DIM)
    positions = jnp.arange(REQ_LEN, dtype=jnp.int32)
    causal = positions[None, :] <= positions[:, None]
    node_rows = jnp.arange(NODE_LEN, dtype=jnp.int32)

    def one_request(inputs):
        query_block, key_block, value_block, leaf = inputs
        middle = parent[leaf]
        ancestry = jnp.stack([leaf, middle, parent[middle]]).astype(jnp.int32)
        key_prefix = prefix_key_nodes[ancestry].reshape(3 * NODE_LEN, HEADS, HEAD_DIM)
        value_prefix = prefix_value_nodes[ancestry].reshape(3 * NODE_LEN, HEADS, HEAD_DIM)
        live_rows = (node_rows[None, :] < node_length[ancestry][:, None]).reshape(3 * NODE_LEN)
        all_keys = jnp.concatenate([key_prefix, key_block], axis=0).astype(jnp.float32)
        all_values = jnp.concatenate([value_prefix, value_block], axis=0).astype(jnp.float32)
        allowed = jnp.concatenate([jnp.broadcast_to(live_rows[None, :], (REQ_LEN, 3 * NODE_LEN)), causal], axis=1)
        allowed = allowed[:, None, :]
        scores = jnp.einsum('qhe,khe->qhk', query_block.astype(jnp.float32), all_keys) * score_scale
        top_score = lax.optimization_barrier(jnp.max(jnp.where(allowed, scores, floor_score), axis=-1, keepdims=True))
        weights = jnp.where(allowed, jnp.exp(scores - top_score), 0.0)
        weight_sum = lax.optimization_barrier(jnp.sum(weights, axis=-1))
        rounded = lax.optimization_barrier(weights.astype(jnp.bfloat16)).astype(jnp.float32)
        summed = jnp.einsum('qhk,khe->qhe', rounded, all_values)
        return (summed / weight_sum[..., None]).astype(jnp.bfloat16)
    attention = lax.map(one_request, (query_req, key_req, value_req, leaf_of_request))
    attention = attention.reshape(TOKENS, HEADS * HEAD_DIM)
    residual = hidden_in.astype(jnp.float32) + jnp.dot(attention, out_weight, preferred_element_type=jnp.float32)
    mean_square = lax.optimization_barrier(jnp.mean(residual * residual, axis=1, keepdims=True))
    normed = (residual * lax.rsqrt(mean_square + epsilon) * norm_gain).astype(jnp.bfloat16)
    groups = TOKENS // TOK_DEV
    route_rows = TOK_DEV * TOPK
    grouped_ids = expert_ids.reshape(groups, route_rows)
    onehot = (grouped_ids[:, :, None] == jnp.arange(EXPERTS, dtype=jnp.int32)[None, None, :]).astype(jnp.int32)
    position = lax.optimization_barrier(jnp.sum((jnp.cumsum(onehot, axis=1) - 1) * onehot, axis=2)).astype(jnp.int32)
    group_grid = jnp.broadcast_to(jnp.arange(groups, dtype=jnp.int32)[:, None], (groups, route_rows))
    token_index = (group_grid * TOK_DEV + jnp.arange(route_rows, dtype=jnp.int32)[None, :] // TOPK).astype(jnp.int32)
    source = jnp.full((EXPERTS, groups, CAP), TOKENS, jnp.int32)
    source = source.at[grouped_ids, group_grid, position].set(token_index)
    source = source.reshape(EXPERTS, groups * CAP)
    slot_index = (group_grid * CAP + position).reshape(TOKENS, TOPK).astype(jnp.int32)
    padded = jnp.concatenate([normed, jnp.zeros((1, D), jnp.bfloat16)], axis=0)
    quarter = FF // N_TENSOR

    def one_expert(running, inputs):
        expert, row_source, weights_gate_up, weights_down = inputs
        slot_rows = padded[row_source]
        gate_part = jnp.dot(slot_rows, weights_gate_up[0], preferred_element_type=jnp.float32)
        up_part = jnp.dot(slot_rows, weights_gate_up[1], preferred_element_type=jnp.float32)
        middle_act = (jax.nn.silu(gate_part) * up_part).astype(jnp.bfloat16)
        expert_out = jnp.zeros((slot_rows.shape[0], D), jnp.float32)
        for quarter_index in range(N_TENSOR):
            partial_out = jnp.dot(middle_act[:, quarter_index * quarter:(quarter_index + 1) * quarter], weights_down[quarter_index * quarter:(quarter_index + 1) * quarter], preferred_element_type=jnp.float32)
            expert_out = expert_out + lax.optimization_barrier(partial_out.astype(jnp.bfloat16)).astype(jnp.float32)
        chosen = expert_ids == expert
        where_slot = lax.optimization_barrier(jnp.sum(jnp.where(chosen, slot_index, 0), axis=1)).astype(jnp.int32)
        route_weight = lax.optimization_barrier(jnp.sum(jnp.where(chosen, gate_weights, 0.0), axis=1))
        return (running + route_weight[:, None] * expert_out[where_slot], None)
    expert_mix, unused = lax.scan(one_expert, jnp.zeros((TOKENS, D), jnp.float32), (jnp.arange(EXPERTS, dtype=jnp.int32), source, gate_up, down_weight))
    return (residual + expert_mix).astype(jnp.bfloat16)
```

```python
import math

import jax
import jax.numpy as jnp
from jax import lax
from jax.experimental import pallas as pl
from jax.experimental.pallas import tpu as pltpu
from jax.sharding import PartitionSpec as P

MESH = pl.DeviceIdType.MESH
D = 2048
HEAD_DIM = 128
REQ_LEN = 64
NODE_LEN = 64
ALL = slice(None)
BF = jnp.bfloat16
F32 = jnp.float32


def dot(a, b):
    return jnp.dot(a, b, preferred_element_type=F32)


def wrap(v, n):
    return lax.rem(v + 4 * n, n)


def kernel(
    leaf_ref, parent_ref, length_ref,
    ids_ref, gate_ref, q_ref, k_ref, v_ref, hidden_ref, gain_ref,
    pk_ref, pv_ref, w_ref, gu_ref, dn_ref,
    out_ref,
    kvbuf, wbuf, gubuf, dnbuf, hbuf, gbuf, psend, precv, resid, xbuf, acc,
    obuf, rbuf, fin, attn,
    send_sems, recv_sems, local_sems,
):
    dp = lax.axis_index("dp")
    e = lax.axis_index("expert")
    t = lax.axis_index("tensor")
    zh, core = dp // 2, lax.rem(dp, 2)
    x, y = e // 4, lax.rem(e, 4)
    z = zh * 4 + t

    def dev(dp_, e_, t_):
        return {"dp": dp_, "expert": e_, "tensor": t_}

    def z_neighbour(step):
        zz = wrap(z + step, 16)
        return dev((zz // 4) * 2 + core, e, lax.rem(zz, 4))

    def x_neighbour(step):
        return dev(dp, wrap(x + step, 4) * 4 + y, t)

    def y_neighbour(step):
        return dev(dp, x * 4 + wrap(y + step, 4), t)

    partner = dev(zh * 2 + (1 - core), e, t)
    z_hi_peers = [dev(wrap(zh + k, 4) * 2 + core, e, t) for k in (1, 2, 3)]
    tensor_ids = [wrap(t + k, 4) for k in (1, 2, 3)]
    tensor_peers = [dev(dp, e, i) for i in tensor_ids]
    expert_ids_of = [wrap(e + k, 16) for k in range(1, 16)]
    expert_peers = [dev(dp, i, t) for i in expert_ids_of]

    barrier = pltpu.get_barrier_semaphore()
    greeted = [partner, z_neighbour(1), z_neighbour(-1)] + z_hi_peers + tensor_peers + expert_peers
    for peer in greeted:
        pl.semaphore_signal(barrier, inc=1, device_id=peer, device_id_type=MESH)

    counts = [0, 0]
    sent = []

    def local(src, dst):
        copy = pltpu.make_async_copy(src, dst, local_sems.at[counts[1]])
        counts[1] += 1
        copy.start()
        return copy

    def remote(src, dst, peer):
        i = counts[0]
        counts[0] += 1
        copy = pltpu.make_async_remote_copy(
            src_ref=src, dst_ref=dst, send_sem=send_sems.at[i], recv_sem=recv_sems.at[i],
            device_id=peer, device_id_type=MESH,
        )
        copy.start()
        sent.append(copy)
        return copy

    def arrived(copies):
        for copy in copies:
            copy.wait_recv()

    def ag_first(view, phase):
        copies = []
        for h in (0, 1):
            p1, p2 = (x, y) if h == 0 else (y, x)
            to = (x_neighbour, y_neighbour)[(h + phase) % 2]
            own = view(h, p1, p2, None) if phase == 0 else view(h, ALL, p2, None)
            for step in (1, -1):
                copies.append(remote(own, own, to(step)))
        return copies

    def ag_second(view, phase):
        copies = []
        for h in (0, 1):
            p1, p2 = (x, y) if h == 0 else (y, x)
            to = (x_neighbour, y_neighbour)[(h + phase) % 2]
            for sub, step in ((0, 1), (1, -1)):
                if phase == 0:
                    slot = view(h, wrap(p1 - step, 4), p2, sub)
                else:
                    slot = view(h, ALL, wrap(p2 - step, 4), sub)
                copies.append(remote(slot, slot, to(step)))
        return copies

    def w_view(h, a1, a2, sub):
        xi, yi = (a1, a2) if h == 0 else (a2, a1)
        rows = pl.ds(h * 256, 256) if sub is None else pl.ds(h * 256 + sub * 128, 128)
        return wbuf.at[xi, yi, rows]

    def kv_view(h, a1, a2, sub):
        xi, yi = (a1, a2) if h == 0 else (a2, a1)
        zs = ALL if sub is None else pl.ds(sub * 2, 2)
        return kvbuf.at[h, zs, core, xi, yi]

    def x_view(h, a1, a2, sub):
        xi, yi = (a1, a2) if h == 0 else (a2, a1)
        cols = ALL if sub is None else pl.ds(sub * 1024, 1024)
        return xbuf.at[xi, yi, pl.ds(h * 16, 16), cols]

    rows16 = pl.ds(pl.multiple_of(e * 16, 16), 16)
    own_w = local(w_ref, wbuf.at[x, y])
    own_kv = [
        local(pk_ref.at[rows16], kvbuf.at[0, zh, core, x, y]),
        local(pv_ref.at[rows16], kvbuf.at[1, zh, core, x, y]),
    ]
    own_rows = pl.ds(pl.multiple_of(t * 32, 32), 32)
    own_small = [
        local(hidden_ref.at[own_rows], hbuf.at[t]),
        local(gain_ref, gbuf.at[t]),
    ]
    own_weights = [local(gu_ref, gubuf.at[t]), local(dn_ref, dnbuf.at[t])]

    pl.semaphore_wait(barrier, len(greeted))

    z_copies = []
    for peer in z_hi_peers:
        z_copies.append(remote(pk_ref.at[rows16], kvbuf.at[0, zh, core, x, y], peer))
        z_copies.append(remote(pv_ref.at[rows16], kvbuf.at[1, zh, core, x, y], peer))
    own_w.wait()
    w_copies = ag_first(w_view, 0)
    small_copies = []
    for i, peer in zip(tensor_ids, tensor_peers):
        rows = pl.ds(pl.multiple_of(i * 32, 32), 32)
        small_copies.append(remote(hidden_ref.at[rows], hbuf.at[t], peer))
        small_copies.append(remote(gain_ref, gbuf.at[t], peer))
    half_rows = pl.ds(pl.multiple_of(core * 128, 128), 128)
    weight_first = []
    for step in (1, -1):
        weight_first.append(remote(gu_ref.at[core], gubuf.at[t, core], z_neighbour(step)))
        weight_first.append(remote(dn_ref.at[half_rows], dnbuf.at[t, half_rows], z_neighbour(step)))

    arrived(w_copies)
    w_copies = ag_second(w_view, 0)
    for copy in own_kv:
        copy.wait()
    arrived(z_copies)
    p_copies = ag_first(kv_view, 0)
    arrived(w_copies)
    w_copies = ag_first(w_view, 1)
    arrived(p_copies)
    p_copies = ag_second(kv_view, 0)
    arrived(p_copies)
    p_copies = ag_first(kv_view, 1)
    arrived(w_copies)
    w_copies = ag_second(w_view, 1)
    arrived(p_copies)
    p_copies = ag_second(kv_view, 1)
    arrived(p_copies)
    partner_kv = [
        remote(kvbuf.at[i, :, core], kvbuf.at[i, :, core], partner) for i in (0, 1)
    ]
    arrived(partner_kv)

    row_id = lax.broadcasted_iota(jnp.int32, (REQ_LEN, 256), 0)
    col_id = lax.broadcasted_iota(jnp.int32, (REQ_LEN, 256), 1)
    in_node = lax.rem(col_id, NODE_LEN)
    piece = col_id // NODE_LEN
    for r in range(2):
        leaf = leaf_ref[r]
        tenant = parent_ref[leaf]
        root = parent_ref[tenant]
        nodes = (leaf, tenant, root)
        limit = jnp.where(
            piece == 0, length_ref[leaf],
            jnp.where(piece == 1, length_ref[tenant],
                      jnp.where(piece == 2, length_ref[root], row_id + 1)),
        )
        allowed = in_node < limit

        def rows_of(i, own):
            parts = [
                kvbuf[i, n // 8, lax.rem(n // 4, 2), lax.rem(n, 4)].reshape(NODE_LEN, 512)
                for n in nodes
            ]
            return jnp.concatenate(parts + [own[r * REQ_LEN:(r + 1) * REQ_LEN]], axis=0)

        keys = rows_of(0, k_ref)
        values = rows_of(1, v_ref)
        for h in range(4):
            cols = slice(h * HEAD_DIM, (h + 1) * HEAD_DIM)
            qh = q_ref[r * REQ_LEN:(r + 1) * REQ_LEN, cols]
            scores = lax.dot_general(
                qh, keys[:, cols], (((1,), (1,)), ((), ())), preferred_element_type=F32
            ) * (1.0 / math.sqrt(HEAD_DIM))
            top = jnp.max(jnp.where(allowed, scores, -1e30), axis=-1, keepdims=True)
            weights = jnp.where(allowed, jnp.exp(scores - top), 0.0)
            total = jnp.sum(weights, axis=-1, keepdims=True)
            summed = dot(weights.astype(BF), values[:, cols])
            attn[r * REQ_LEN:(r + 1) * REQ_LEN, cols] = (summed / total).astype(BF)

    arrived(w_copies)
    for i in range(16):
        part = dot(attn[...], wbuf[i // 4, i % 4]).astype(BF)
        psend[:, :, i * 128:(i + 1) * 128] = part.reshape(4, 32, 128)
    proj_copies = [
        remote(psend.at[i], precv.at[t], peer) for i, peer in zip(tensor_ids, tensor_peers)
    ]
    arrived(weight_first)
    weight_second = []
    for sub, step in ((0, 1), (1, -1)):
        slot = wrap(t - step, 4)
        rows = pl.ds(sub * 1024, 1024)
        a = gubuf.at[slot, core, rows]
        b = dnbuf.at[slot, half_rows, rows]
        weight_second.append(remote(a, a, z_neighbour(step)))
        weight_second.append(remote(b, b, z_neighbour(step)))
    partner_w = []
    for step in (1, -1):
        slot = wrap(t - step, 4)
        a = gubuf.at[slot, core]
        b = dnbuf.at[slot, half_rows]
        partner_w.append(remote(a, a, partner))
        partner_w.append(remote(b, b, partner))
    for copy in own_small:
        copy.wait()
    arrived(small_copies)
    arrived(proj_copies)

    square = jnp.zeros((32, 1), F32)
    for j in range(4):
        cols = slice(j * 512, (j + 1) * 512)
        total = psend[t, :, cols].astype(F32)
        for i in tensor_ids:
            total = total + precv[i, :, cols].astype(F32)
        total = total + hbuf[j].astype(F32)
        resid[:, cols] = total
        square = square + jnp.sum(total * total, axis=1, keepdims=True)
    factor = lax.rsqrt(square / D + 1e-05)
    for j in range(4):
        cols = slice(j * 512, (j + 1) * 512)
        xbuf[x, y, :, cols] = (resid[:, cols] * factor * gbuf[j, 0:1]).astype(BF)

    x_copies = ag_first(x_view, 0)
    arrived(x_copies)
    x_copies = ag_second(x_view, 0)
    arrived(x_copies)
    x_copies = ag_first(x_view, 1)
    arrived(x_copies)
    x_copies = ag_second(x_view, 1)
    arrived(weight_second)
    opposite = wrap(t + 2, 4)
    a = gubuf.at[opposite, core]
    b = dnbuf.at[opposite, half_rows]
    partner_w.append(remote(a, a, partner))
    partner_w.append(remote(b, b, partner))
    for copy in own_weights:
        copy.wait()
    arrived(x_copies)
    arrived(partner_w)

    acc[...] = jnp.zeros_like(acc)

    def quarter(j, carry):
        def block(m, c):
            tokens = xbuf[pl.ds(2 * m, 2)].reshape(256, D)
            gate = dot(tokens, gubuf[j, 0])
            up = dot(tokens, gubuf[j, 1])
            middle = (gate * jax.nn.sigmoid(gate) * up).astype(BF)
            for n in range(4):
                cols = slice(n * 512, (n + 1) * 512)
                acc[pl.ds(8 * m, 8), :, cols] += dot(middle, dnbuf[j, :, cols]).reshape(8, 32, 512)
            return c

        return lax.fori_loop(0, 2, block, carry)

    lax.fori_loop(0, 4, quarter, 0)
    obuf[...] = acc[...].astype(BF)
    back = [remote(obuf.at[i], rbuf.at[e], peer) for i, peer in zip(expert_ids_of, expert_peers)]
    arrived(back)

    ids = ids_ref[pl.ds(pl.multiple_of(t * 32, 32), 32)]
    gates = gate_ref[pl.ds(pl.multiple_of(t * 32, 32), 32)]
    mix_weights = [
        jnp.sum(jnp.where(ids == i, gates, 0.0), axis=1, keepdims=True) for i in range(16)
    ]
    own_weight = jnp.sum(jnp.where(ids == e, gates, 0.0), axis=1, keepdims=True)
    rbuf[e] = jnp.zeros((32, D), BF)
    for j in range(4):
        cols = slice(j * 512, (j + 1) * 512)
        total = resid[:, cols] + own_weight * obuf[e, :, cols].astype(F32)
        for i in range(16):
            total = total + mix_weights[i] * rbuf[i, :, cols].astype(F32)
        fin[j] = total.astype(BF)
    out_copies = [
        remote(fin.at[i], out_ref.at[own_rows], peer) for i, peer in zip(tensor_ids, tensor_peers)
    ]
    last = local(fin.at[t], out_ref.at[own_rows])
    last.wait()
    arrived(out_copies)
    for copy in sent:
        copy.wait_send()


def body(
    hidden_in, queries, new_keys, new_values, prefix_keys, prefix_values, node_length, parent,
    leaf_of_request, out_weight, norm_gain, expert_ids, gate_weights, gate_up, down_weight,
):
    smem = pl.BlockSpec(memory_space=pltpu.SMEM)
    vmem = pl.BlockSpec(memory_space=pltpu.VMEM)
    hbm = pl.BlockSpec(memory_space=pl.ANY)
    gain = jnp.broadcast_to(norm_gain[None, :], (8, norm_gain.shape[0]))
    return pl.pallas_call(
        kernel,
        out_shape=jax.ShapeDtypeStruct(hidden_in.shape, BF),
        in_specs=[smem] * 3 + [vmem] * 7 + [hbm] * 5,
        out_specs=vmem,
        scratch_shapes=[
            pltpu.VMEM((2, 4, 2, 4, 4, 16, 512), BF),
            pltpu.VMEM((4, 4, 512, 128), BF),
            pltpu.VMEM((4, 2, 2048, 256), BF),
            pltpu.VMEM((4, 256, 2048), BF),
            pltpu.VMEM((4, 32, 512), BF),
            pltpu.VMEM((4, 8, 512), F32),
            pltpu.VMEM((4, 32, 2048), BF),
            pltpu.VMEM((4, 32, 2048), BF),
            pltpu.VMEM((32, 2048), F32),
            pltpu.VMEM((4, 4, 32, 2048), BF),
            pltpu.VMEM((16, 32, 2048), F32),
            pltpu.VMEM((16, 32, 2048), BF),
            pltpu.VMEM((16, 32, 2048), BF),
            pltpu.VMEM((4, 32, 512), BF),
            pltpu.VMEM((128, 512), BF),
            pltpu.SemaphoreType.DMA((112,)),
            pltpu.SemaphoreType.DMA((112,)),
            pltpu.SemaphoreType.DMA((16,)),
        ],
        compiler_params=pltpu.CompilerParams(
            collective_id=0, has_side_effects=True, vmem_limit_bytes=56 << 20
        ),
        name="layer",
    )(
        leaf_of_request, parent, node_length, expert_ids, gate_weights, queries, new_keys,
        new_values, hidden_in, gain, prefix_keys, prefix_values, out_weight, gate_up[0],
        down_weight[0],
    )


def solution(mesh):
    rows = P(("dp", "expert"), "tensor")
    placed = (
        rows, rows, rows, rows,
        P("dp", "tensor"),
        P("dp", "tensor"),
        P(), P(),
        P(("dp", "expert")),
        P("tensor", "expert"),
        P("tensor"),
        P(("dp", "expert"), None),
        P(("dp", "expert"), None),
        P("expert", None, None, "tensor"),
        P("expert", "tensor", None),
    )
    return jax.shard_map(body, mesh=mesh, in_specs=placed, out_specs=rows, check_vma=False)
```

```python
import math

import jax
import jax.numpy as jnp
from jax import lax
from jax.experimental import pallas as pl
from jax.experimental.pallas import tpu as pltpu
from jax.sharding import PartitionSpec as P

MESH = pl.DeviceIdType.MESH
D = 2048
HEAD_DIM = 128
REQ_LEN = 64
NODE_LEN = 64
ALL = slice(None)
BF = jnp.bfloat16
F32 = jnp.float32


def dot(a, b):
    return jnp.dot(a, b, preferred_element_type=F32)


def wrap(v, n):
    return lax.rem(v + 4 * n, n)


def kernel(
    leaf_ref, parent_ref, length_ref,
    ids_ref, gate_ref, q_ref, k_ref, v_ref, hidden_ref, gain_ref,
    pk_ref, pv_ref, w_ref, gu_ref, dn_ref,
    out_ref,
    kvbuf, wbuf, gubuf, dnbuf, hbuf, gbuf, psend, precv, resid, xbuf, acc,
    obuf, fin, attn, routes, far_near, far_sum, near_half, near_sum, row_sum,
    send_sems, recv_sems, local_sems,
):
    dp = lax.axis_index("dp")
    e = lax.axis_index("expert")
    t = lax.axis_index("tensor")
    zh, core = dp // 2, lax.rem(dp, 2)
    x, y = e // 4, lax.rem(e, 4)
    z = zh * 4 + t

    def dev(dp_, e_, t_):
        return {"dp": dp_, "expert": e_, "tensor": t_}

    def z_neighbour(step):
        zz = wrap(z + step, 16)
        return dev((zz // 4) * 2 + core, e, lax.rem(zz, 4))

    def x_neighbour(step):
        return dev(dp, wrap(x + step, 4) * 4 + y, t)

    def y_neighbour(step):
        return dev(dp, x * 4 + wrap(y + step, 4), t)

    partner = dev(zh * 2 + (1 - core), e, t)
    tensor_ids = [wrap(t + k, 4) for k in (1, 2, 3)]
    tensor_peers = [dev(dp, e, i) for i in tensor_ids]

    def z_hi_neighbour(step):
        return dev(wrap(zh + step, 4) * 2 + core, e, t)

    barrier = pltpu.get_barrier_semaphore()
    greeted = [partner] + tensor_peers
    for to in (x_neighbour, y_neighbour, z_neighbour, z_hi_neighbour):
        greeted += [to(1), to(-1)]
    for peer in greeted:
        pl.semaphore_signal(barrier, inc=1, device_id=peer, device_id_type=MESH)

    counts = [0, 0]
    sent = []

    def local(src, dst):
        copy = pltpu.make_async_copy(src, dst, local_sems.at[counts[1]])
        counts[1] += 1
        copy.start()
        return copy

    def remote(src, dst, peer):
        i = counts[0]
        counts[0] += 1
        copy = pltpu.make_async_remote_copy(
            src_ref=src, dst_ref=dst, send_sem=send_sems.at[i], recv_sem=recv_sems.at[i],
            device_id=peer, device_id_type=MESH,
        )
        copy.start()
        sent.append(copy)
        return copy

    def arrived(copies):
        for copy in copies:
            copy.wait_recv()

    def ag_first(view, phase):
        copies = []
        for h in (0, 1):
            p1, p2 = (x, y) if h == 0 else (y, x)
            to = (x_neighbour, y_neighbour)[(h + phase) % 2]
            own = view(h, p1, p2, None) if phase == 0 else view(h, ALL, p2, None)
            for step in (1, -1):
                copies.append(remote(own, own, to(step)))
        return copies

    def ag_second(view, phase):
        copies = []
        for h in (0, 1):
            p1, p2 = (x, y) if h == 0 else (y, x)
            to = (x_neighbour, y_neighbour)[(h + phase) % 2]
            for sub, step in ((0, 1), (1, -1)):
                if phase == 0:
                    slot = view(h, wrap(p1 - step, 4), p2, sub)
                else:
                    slot = view(h, ALL, wrap(p2 - step, 4), sub)
                copies.append(remote(slot, slot, to(step)))
        return copies

    def w_view(h, a1, a2, sub):
        xi, yi = (a1, a2) if h == 0 else (a2, a1)
        start = core * 256 + h * 128
        rows = pl.ds(start, 128) if sub is None else pl.ds(start + sub * 64, 64)
        return wbuf.at[xi, yi, rows]

    def kv_view(h, a1, a2, sub):
        xi, yi = (a1, a2) if h == 0 else (a2, a1)
        zs = ALL if sub is None else pl.ds(sub * 2, 2)
        return kvbuf.at[h, zs, core, xi, yi]

    def x_view(h, a1, a2, sub):
        xi, yi = (a1, a2) if h == 0 else (a2, a1)
        cols = ALL if sub is None else (pl.ds(0, 1152), pl.ds(1152, 1024))[sub]
        return xbuf.at[xi, yi, pl.ds(h * 16, 16), cols]

    rows16 = pl.ds(pl.multiple_of(e * 16, 16), 16)
    w_rows = pl.ds(pl.multiple_of(core * 256, 256), 256)
    own_w = local(w_ref.at[w_rows], wbuf.at[x, y, w_rows])
    own_kv = [
        local(pk_ref.at[rows16], kvbuf.at[0, zh, core, x, y]),
        local(pv_ref.at[rows16], kvbuf.at[1, zh, core, x, y]),
    ]
    own_rows = pl.ds(pl.multiple_of(t * 32, 32), 32)
    own_small = [
        local(hidden_ref.at[own_rows], hbuf.at[t]),
        local(gain_ref, gbuf.at[t]),
    ]
    own_weights = [local(gu_ref, gubuf.at[t]), local(dn_ref, dnbuf.at[t])]

    routes[0] = ids_ref[...].astype(F32).T
    routes[1] = gate_ref[...].T
    named, gates = routes[0, own_rows], routes[1, own_rows]
    lane = lax.broadcasted_iota(jnp.int32, (32, 128), 1)
    lane_expert = jnp.where(lane < 48, lax.rem(lane, 16), -1).astype(F32)
    weight = jnp.zeros((32, 128), F32)
    for i in range(8):
        weight = weight + jnp.where(lane_expert == named[:, i:i + 1], gates[:, i:i + 1], 0.0)
    high = weight.astype(BF)
    rest = weight - high.astype(F32)
    middle = rest.astype(BF)
    low = (rest - middle.astype(F32)).astype(BF)
    xbuf[x, y, :, 2048:] = jnp.where(lane < 16, high, jnp.where(lane < 32, middle, low))

    pl.semaphore_wait(barrier, len(greeted))

    z_copies = []
    for step in (1, -1):
        for i, ref in ((0, pk_ref), (1, pv_ref)):
            z_copies.append(
                remote(ref.at[rows16], kvbuf.at[i, zh, core, x, y], z_hi_neighbour(step))
            )
    own_w.wait()
    w_copies = ag_first(w_view, 0)
    half_rows = pl.ds(pl.multiple_of(core * 128, 128), 128)
    up_first = [remote(gu_ref.at[core], gubuf.at[t, core], z_neighbour(k)) for k in (1, -1)]
    down_first = [
        remote(dn_ref.at[half_rows], dnbuf.at[t, half_rows], z_neighbour(k)) for k in (1, -1)
    ]
    small_copies = []
    for i, peer in zip(tensor_ids, tensor_peers):
        rows = pl.ds(pl.multiple_of(i * 32, 32), 32)
        small_copies.append(remote(hidden_ref.at[rows], hbuf.at[t], peer))
        small_copies.append(remote(gain_ref, gbuf.at[t], peer))

    def to_partner(view, phase, stage):
        copies = []
        for h in (0, 1):
            p2 = y if h == 0 else x
            for step in ((0,), (1, -1), (2,))[stage]:
                slot = view(h, ALL, wrap(p2 + step, 4), None)
                copies.append(remote(slot, slot, partner))
        return copies

    arrived(z_copies)
    z_copies = []
    for i, step in ((0, 1), (1, -1)):
        slot = kvbuf.at[i, wrap(zh - step, 4), core, x, y]
        z_copies.append(remote(slot, slot, z_hi_neighbour(step)))
    for copy in own_kv:
        copy.wait()
    arrived(w_copies)
    w_copies = ag_second(w_view, 0)
    arrived(z_copies)
    p_copies = ag_first(kv_view, 0)
    arrived(w_copies)
    w_copies = ag_first(w_view, 1)
    w_partner = to_partner(w_view, 1, 0)
    arrived(p_copies)
    p_copies = ag_second(kv_view, 0)
    arrived(p_copies)
    p_copies = ag_first(kv_view, 1)
    p_partner = to_partner(kv_view, 1, 0)
    arrived(w_copies)
    w_copies = ag_second(w_view, 1)
    w_partner += to_partner(w_view, 1, 1)
    arrived(p_copies)
    p_copies = ag_second(kv_view, 1)
    p_partner += to_partner(kv_view, 1, 1)
    arrived(w_copies)
    w_partner += to_partner(w_view, 1, 2)
    arrived(p_copies)
    p_partner += to_partner(kv_view, 1, 2)

    def pass_on(arrivals, views):
        arrived(arrivals)
        on, across = [], []
        for sub, step in ((0, 1), (1, -1)):
            slot = wrap(t - step, 4)
            part = views(slot, sub)
            on.append(remote(part, part, z_neighbour(step)))
            whole = views(slot, None)
            across.append(remote(whole, whole, partner))
        return on, across

    def up_view(slot, sub):
        return gubuf.at[slot, core, ALL if sub is None else pl.ds(sub * 1024, 1024)]

    def down_view(slot, sub):
        return dnbuf.at[slot, half_rows, ALL if sub is None else pl.ds(sub * 1024, 1024)]

    up_second, up_across = pass_on(up_first, up_view)
    arrived(p_partner)

    row_id = lax.broadcasted_iota(jnp.int32, (REQ_LEN, 256), 0)
    col_id = lax.broadcasted_iota(jnp.int32, (REQ_LEN, 256), 1)
    in_node = lax.rem(col_id, NODE_LEN)
    piece = col_id // NODE_LEN
    for r in range(2):
        leaf = leaf_ref[r]
        tenant = parent_ref[leaf]
        root = parent_ref[tenant]
        nodes = (leaf, tenant, root)
        limit = jnp.where(
            piece == 0, length_ref[leaf],
            jnp.where(piece == 1, length_ref[tenant],
                      jnp.where(piece == 2, length_ref[root], row_id + 1)),
        )
        allowed = in_node < limit

        def rows_of(i, own):
            parts = [
                kvbuf[i, n // 8, lax.rem(n // 4, 2), lax.rem(n, 4)].reshape(NODE_LEN, 512)
                for n in nodes
            ]
            return jnp.concatenate(parts + [own[r * REQ_LEN:(r + 1) * REQ_LEN]], axis=0)

        keys = rows_of(0, k_ref)
        values = rows_of(1, v_ref)
        for h in range(4):
            cols = slice(h * HEAD_DIM, (h + 1) * HEAD_DIM)
            qh = q_ref[r * REQ_LEN:(r + 1) * REQ_LEN, cols]
            scores = lax.dot_general(
                qh, keys[:, cols], (((1,), (1,)), ((), ())), preferred_element_type=F32
            ) * (1.0 / math.sqrt(HEAD_DIM))
            top = jnp.max(jnp.where(allowed, scores, -1e30), axis=-1, keepdims=True)
            weights = jnp.where(allowed, jnp.exp(scores - top), 0.0)
            total = jnp.sum(weights, axis=-1, keepdims=True)
            summed = dot(weights.astype(BF), values[:, cols])
            attn[r * REQ_LEN:(r + 1) * REQ_LEN, cols] = (summed / total).astype(BF)

    arrived(w_partner)
    for i in range(16):
        part = dot(attn[...], wbuf[i // 4, i % 4]).astype(BF)
        psend[:, :, i * 128:(i + 1) * 128] = part.reshape(4, 32, 128)
    proj_copies = [
        remote(psend.at[i], precv.at[t], peer) for i, peer in zip(tensor_ids, tensor_peers)
    ]
    down_second, down_across = pass_on(down_first, down_view)
    for copy in own_small:
        copy.wait()
    arrived(small_copies)
    arrived(proj_copies)

    square = jnp.zeros((32, 1), F32)
    for j in range(4):
        cols = slice(j * 512, (j + 1) * 512)
        total = psend[t, :, cols].astype(F32)
        for i in tensor_ids:
            total = total + precv[i, :, cols].astype(F32)
        total = total + hbuf[j].astype(F32)
        resid[:, cols] = total
        square = square + jnp.sum(total * total, axis=1, keepdims=True)
    factor = lax.rsqrt(square / D + 1e-05)
    for j in range(4):
        cols = slice(j * 512, (j + 1) * 512)
        xbuf[x, y, :, cols] = (resid[:, cols] * factor * gbuf[j]).astype(BF)

    x_copies = ag_first(x_view, 0)
    arrived(x_copies)
    x_copies = ag_second(x_view, 0)
    arrived(x_copies)
    x_copies = ag_first(x_view, 1)
    arrived(x_copies)
    x_copies = ag_second(x_view, 1)
    for copy in own_weights:
        copy.wait()
    arrived(x_copies)

    def quarter(slot, place):
        def block(m, c):
            tokens = xbuf[pl.ds(2 * m, 2), :, :, 0:D].reshape(256, D)
            gate = dot(tokens, gubuf[slot, 0])
            up = dot(tokens, gubuf[slot, 1])
            hidden = (gate * jax.nn.sigmoid(gate) * up).astype(BF)
            lanes = lax.broadcasted_iota(jnp.int32, (256, 128), 1)
            parts = xbuf[pl.ds(2 * m, 2), :, :, D:].reshape(256, 128).astype(F32)
            route = jnp.sum(
                jnp.where(lax.rem(lanes, 16) == e, parts, 0.0), axis=1, keepdims=True
            )
            for n in range(4):
                cols = slice(n * 512, (n + 1) * 512)
                here = (pl.ds(2 * m, 2), ALL, ALL, cols)
                part = dot(hidden, dnbuf[slot, :, cols])
                if place != "first":
                    part = part + acc[here].reshape(256, 512)
                if place == "last":
                    obuf[here] = (part * route).astype(BF).reshape(2, 4, 32, 512)
                else:
                    acc[here] = part.reshape(2, 4, 32, 512)
            return c

        lax.fori_loop(0, 2, block, 0)

    quarter(t, "first")
    arrived(up_across)
    arrived(down_across)

    def side(i, c):
        quarter(wrap(t + 1 + 2 * i, 4), "next")
        return c

    lax.fori_loop(0, 2, side, 0)
    opposite = wrap(t + 2, 4)
    last_across = []
    arrived(up_second)
    last_across.append(remote(up_view(opposite, None), up_view(opposite, None), partner))
    arrived(down_second)
    last_across.append(remote(down_view(opposite, None), down_view(opposite, None), partner))
    arrived(last_across)
    quarter(opposite, "last")

    col_halves = (slice(0, 1024), slice(1024, 2048))

    def exchange(to, at, rs_half, rs_full, h):
        def go(phase, pending):
            arrived(pending)
            if phase == 0:
                return [
                    remote(at(2, col_halves[i]), rs_half.at[h, i], to(step))
                    for i, step in ((0, 1), (1, -1))
                ]
            for i, step in ((0, 1), (1, -1)):
                ref = at(step, col_halves[i])
                ref[...] = (ref[...].astype(F32) + rs_half[h, i].astype(F32)).astype(BF)
            return [
                remote(at(step, ALL), rs_full.at[h, i], to(step))
                for i, step in ((0, 1), (1, -1))
            ]

        return go

    rows_of_half = (slice(0, 16), slice(16, 32))

    def far_at(h):
        def at(step, cols):
            if h == 0:
                return obuf.at[ALL, wrap(y + step, 4), rows_of_half[0], cols]
            return obuf.at[wrap(x + step, 4), ALL, rows_of_half[1], cols]

        return at

    def near_at(h):
        def at(step, cols):
            return row_sum.at[h, wrap((x, y)[h] + step, 4), ALL, cols]

        return at

    far = [exchange((y_neighbour, x_neighbour)[h], far_at(h), far_near, far_sum, h) for h in (0, 1)]
    near = [exchange((x_neighbour, y_neighbour)[h], near_at(h), near_half, near_sum, h) for h in (0, 1)]
    pending = [far[h](0, []) for h in (0, 1)]
    pending = [far[h](1, pending[h]) for h in (0, 1)]
    after = []
    for h in (0, 1):
        arrived(pending[h])
        total = far_at(h)(0, ALL)[...].astype(F32)
        total = total + far_sum[h, 0].astype(F32) + far_sum[h, 1].astype(F32)
        row_sum[h] = total.astype(BF)
        after.append(near[h](0, []))
    after = [near[h](1, after[h]) for h in (0, 1)]
    for h in (0, 1):
        arrived(after[h])
        for j in range(4):
            cols = slice(j * 512, (j + 1) * 512)
            total = resid[rows_of_half[h], cols] + near_at(h)(0, cols)[...].astype(F32)
            total = total + near_sum[h, 0, :, cols].astype(F32) + near_sum[h, 1, :, cols].astype(F32)
            fin[j, rows_of_half[h]] = total.astype(BF)
    out_copies = [
        remote(fin.at[i], out_ref.at[own_rows], peer) for i, peer in zip(tensor_ids, tensor_peers)
    ]
    last = local(fin.at[t], out_ref.at[own_rows])
    last.wait()
    arrived(out_copies)
    for copy in sent:
        copy.wait_send()


def body(
    hidden_in, queries, new_keys, new_values, prefix_keys, prefix_values, node_length, parent,
    leaf_of_request, out_weight, norm_gain, expert_ids, gate_weights, gate_up, down_weight,
):
    smem = pl.BlockSpec(memory_space=pltpu.SMEM)
    vmem = pl.BlockSpec(memory_space=pltpu.VMEM)
    hbm = pl.BlockSpec(memory_space=pl.ANY)
    return pl.pallas_call(
        kernel,
        out_shape=jax.ShapeDtypeStruct(hidden_in.shape, BF),
        in_specs=[smem] * 3 + [vmem] * 7 + [hbm] * 5,
        out_specs=vmem,
        scratch_shapes=[
            pltpu.VMEM((2, 4, 2, 4, 4, 16, 512), BF),
            pltpu.VMEM((4, 4, 512, 128), BF),
            pltpu.VMEM((4, 2, 2048, 256), BF),
            pltpu.VMEM((4, 256, 2048), BF),
            pltpu.VMEM((4, 32, 512), BF),
            pltpu.VMEM((4, 1, 512), F32),
            pltpu.VMEM((4, 32, 2048), BF),
            pltpu.VMEM((4, 32, 2048), BF),
            pltpu.VMEM((32, 2048), F32),
            pltpu.VMEM((4, 4, 32, 2176), BF),
            pltpu.VMEM((4, 4, 32, 2048), F32),
            pltpu.VMEM((4, 4, 32, 2048), BF),
            pltpu.VMEM((4, 32, 512), BF),
            pltpu.VMEM((128, 512), BF),
            pltpu.VMEM((2, 128, 8), F32),
            pltpu.VMEM((2, 2, 4, 16, 1024), BF),
            pltpu.VMEM((2, 2, 4, 16, 2048), BF),
            pltpu.VMEM((2, 2, 16, 1024), BF),
            pltpu.VMEM((2, 2, 16, 2048), BF),
            pltpu.VMEM((2, 4, 16, 2048), BF),
            pltpu.SemaphoreType.DMA((128,)),
            pltpu.SemaphoreType.DMA((128,)),
            pltpu.SemaphoreType.DMA((16,)),
        ],
        compiler_params=pltpu.CompilerParams(
            collective_id=0, has_side_effects=True, vmem_limit_bytes=56 << 20
        ),
        name="layer",
    )(
        leaf_of_request, parent, node_length, expert_ids.T, gate_weights.T, queries, new_keys,
        new_values, hidden_in, norm_gain[None, :], prefix_keys, prefix_values, out_weight, gate_up[0],
        down_weight[0],
    )


def solution(mesh):
    rows = P(("dp", "expert"), "tensor")
    placed = (
        rows, rows, rows, rows,
        P("dp", "tensor"),
        P("dp", "tensor"),
        P(), P(),
        P(("dp", "expert")),
        P("tensor", "expert"),
        P("tensor"),
        P(("dp", "expert"), None),
        P(("dp", "expert"), None),
        P("expert", None, None, "tensor"),
        P("expert", "tensor", None),
    )
    return jax.shard_map(body, mesh=mesh, in_specs=placed, out_specs=rows, check_vma=False)
```

```python
import math

import jax
import jax.numpy as jnp
from jax import lax
from jax.experimental import pallas as pl
from jax.experimental.pallas import tpu as pltpu
from jax.sharding import PartitionSpec as P

MESH = pl.DeviceIdType.MESH
D = 2048
HEAD_DIM = 128
REQ_LEN = 64
NODE_LEN = 64
ALL = slice(None)
BF = jnp.bfloat16
F32 = jnp.float32


def dot(a, b):
    return jnp.dot(a, b, preferred_element_type=F32)


def wrap(v, n):
    return lax.rem(v + 4 * n, n)


def kernel(
    leaf_ref, parent_ref, length_ref,
    ids_ref, gate_ref, q_ref, k_ref, v_ref, hidden_ref, gain_ref,
    pk_ref, pv_ref, w_ref, gu_ref, dn_ref,
    out_ref,
    kvbuf, wbuf, gubuf, dnbuf, hbuf, gbuf, psend, precv, resid, xbuf, xrow, acc,
    obuf, fin, attn, routes, far_near, far_sum, near_half, near_sum, row_sum,
    send_sems, recv_sems, local_sems,
):
    dp = lax.axis_index("dp")
    e = lax.axis_index("expert")
    t = lax.axis_index("tensor")
    zh, core = dp // 2, lax.rem(dp, 2)
    x, y = e // 4, lax.rem(e, 4)
    z = zh * 4 + t

    def dev(dp_, e_, t_):
        return {"dp": dp_, "expert": e_, "tensor": t_}

    def z_neighbour(step):
        zz = wrap(z + step, 16)
        return dev((zz // 4) * 2 + core, e, lax.rem(zz, 4))

    def x_neighbour(step):
        return dev(dp, wrap(x + step, 4) * 4 + y, t)

    def y_neighbour(step):
        return dev(dp, x * 4 + wrap(y + step, 4), t)

    partner = dev(zh * 2 + (1 - core), e, t)
    tensor_ids = [wrap(t + k, 4) for k in (1, 2, 3)]
    tensor_peers = [dev(dp, e, i) for i in tensor_ids]

    def z_hi_neighbour(step):
        return dev(wrap(zh + step, 4) * 2 + core, e, t)

    barrier = pltpu.get_barrier_semaphore()
    greeted = [partner] + tensor_peers
    for to in (x_neighbour, y_neighbour, z_neighbour, z_hi_neighbour):
        greeted += [to(1), to(-1)]
    for peer in greeted:
        pl.semaphore_signal(barrier, inc=1, device_id=peer, device_id_type=MESH)

    counts = [0, 0]
    sent = []

    def local(src, dst):
        copy = pltpu.make_async_copy(src, dst, local_sems.at[counts[1]])
        counts[1] += 1
        copy.start()
        return copy

    def remote(src, dst, peer):
        i = counts[0]
        counts[0] += 1
        copy = pltpu.make_async_remote_copy(
            src_ref=src, dst_ref=dst, send_sem=send_sems.at[i], recv_sem=recv_sems.at[i],
            device_id=peer, device_id_type=MESH,
        )
        copy.start()
        sent.append(copy)
        return copy

    def arrived(copies):
        for copy in copies:
            copy.wait_recv()

    def ag_first(view, phase):
        copies = []
        for h in (0, 1):
            p1, p2 = (x, y) if h == 0 else (y, x)
            to = (x_neighbour, y_neighbour)[(h + phase) % 2]
            own = view(h, p1, p2, None) if phase == 0 else view(h, ALL, p2, None)
            for step in (1, -1):
                copies.append(remote(own, own, to(step)))
        return copies

    def ag_second(view, phase):
        copies = []
        for h in (0, 1):
            p1, p2 = (x, y) if h == 0 else (y, x)
            to = (x_neighbour, y_neighbour)[(h + phase) % 2]
            for sub, step in ((0, 1), (1, -1)):
                if phase == 0:
                    slot = view(h, wrap(p1 - step, 4), p2, sub)
                else:
                    slot = view(h, ALL, wrap(p2 - step, 4), sub)
                copies.append(remote(slot, slot, to(step)))
        return copies

    def w_view(h, a1, a2, sub):
        xi, yi = (a1, a2) if h == 0 else (a2, a1)
        start = core * 256 + h * 128
        rows = pl.ds(start, 128) if sub is None else pl.ds(start + sub * 64, 64)
        return wbuf.at[xi, yi, rows]

    def kv_view(zs):
        def view(h, a1, a2, sub):
            xi, yi = (a1, a2) if h == 0 else (a2, a1)
            cols = ALL if sub is None else pl.ds(sub * 256, 256)
            return kvbuf.at[h, zs, core, xi, yi, ALL, cols]

        return view

    def gather(view, done):
        for phase in (0, 1):
            copies = ag_first(view, phase)
            yield
            arrived(copies)
            copies = ag_second(view, phase)
            yield
            arrived(copies)
        done()
        yield

    rows16 = pl.ds(pl.multiple_of(e * 16, 16), 16)
    w_rows = pl.ds(pl.multiple_of(core * 256, 256), 256)
    own_w = local(w_ref.at[w_rows], wbuf.at[x, y, w_rows])
    own_kv = [
        local(pk_ref.at[rows16], kvbuf.at[0, zh, core, x, y]),
        local(pv_ref.at[rows16], kvbuf.at[1, zh, core, x, y]),
    ]
    own_rows = pl.ds(pl.multiple_of(t * 32, 32), 32)
    own_small = [
        local(hidden_ref.at[own_rows], hbuf.at[t]),
        local(gain_ref, gbuf.at[t]),
    ]
    own_weights = [local(gu_ref, gubuf.at[t]), local(dn_ref, dnbuf.at[t])]

    routes[0] = ids_ref[...].astype(F32).T
    routes[1] = gate_ref[...].T
    named, gates = routes[0, own_rows], routes[1, own_rows]
    lane = lax.broadcasted_iota(jnp.int32, (32, 128), 1)
    lane_expert = jnp.where(lane < 48, lax.rem(lane, 16), -1).astype(F32)
    weight = jnp.zeros((32, 128), F32)
    for i in range(8):
        weight = weight + jnp.where(lane_expert == named[:, i:i + 1], gates[:, i:i + 1], 0.0)
    high = weight.astype(BF)
    rest = weight - high.astype(F32)
    middle = rest.astype(BF)
    low = (rest - middle.astype(F32)).astype(BF)
    routed = jnp.where(lane < 16, high, jnp.where(lane < 32, middle, low))
    firsts, seconds = (x, y), (y, x)
    for h in (0, 1):
        xbuf[h, firsts[h], seconds[h], :, D:] = routed[h * 16:(h + 1) * 16]
    acc[...] = jnp.zeros_like(acc)

    pl.semaphore_wait(barrier, len(greeted))

    z_copies = []
    for step in (1, -1):
        for i, ref in ((0, pk_ref), (1, pv_ref)):
            z_copies.append(
                remote(ref.at[rows16], kvbuf.at[i, zh, core, x, y], z_hi_neighbour(step))
            )
    for copy in own_kv:
        copy.wait()
    p_partner, w_partner = [], []

    def prefix_gather(zs):
        def done():
            for i in (0, 1):
                piece = kvbuf.at[i, zs, core]
                p_partner.append(remote(piece, piece, partner))

        return gather(kv_view(zs), done)

    def w_done():
        rows = wbuf.at[:, :, w_rows]
        w_partner.append(remote(rows, rows, partner))

    mine, w_all = prefix_gather(zh), gather(w_view, w_done)
    next(mine)
    own_w.wait()
    next(w_all)
    half_rows = pl.ds(pl.multiple_of(core * 128, 128), 128)

    def up_rows(start, size):
        rows = pl.ds(start, size)
        return [
            remote(gu_ref.at[core, rows], gubuf.at[t, core, rows], z_neighbour(k)) for k in (1, -1)
        ]

    up_first = up_rows(0, 256)

    next(mine)
    next(w_all)
    arrived(z_copies)
    z_copies = []
    for i, step in ((0, 1), (1, -1)):
        slot = kvbuf.at[i, wrap(zh - step, 4), core, x, y]
        z_copies.append(remote(slot, slot, z_hi_neighbour(step)))
    up_first += up_rows(256, 1792)
    small_copies = []
    for i, peer in zip(tensor_ids, tensor_peers):
        rows = pl.ds(pl.multiple_of(i * 32, 32), 32)
        small_copies.append(remote(hidden_ref.at[rows], hbuf.at[t], peer))
        small_copies.append(remote(gain_ref, gbuf.at[t], peer))
    before, behind = prefix_gather(wrap(zh - 1, 4)), prefix_gather(wrap(zh + 1, 4))
    next(before)
    next(behind)
    next(mine)
    next(w_all)
    next(before)
    next(behind)
    next(mine)
    arrived(z_copies)
    across = prefix_gather(wrap(zh + 2, 4))
    next(across)
    next(w_all)
    next(before)
    next(behind)
    next(mine)
    next(across)
    next(before)
    next(behind)
    next(w_all)
    next(across)
    next(before)
    next(behind)
    next(across)
    next(across)

    def pass_on(arrivals, views):
        arrived(arrivals)
        on, across = [], []
        for sub, step in ((0, 1), (1, -1)):
            slot = wrap(t - step, 4)
            part = views(slot, sub)
            on.append(remote(part, part, z_neighbour(step)))
            whole = views(slot, None)
            across.append(remote(whole, whole, partner))
        return on, across

    def up_view(slot, sub):
        return gubuf.at[slot, core, ALL if sub is None else pl.ds(sub * 1024, 1024)]

    def down_view(slot, sub):
        return dnbuf.at[slot, half_rows, ALL if sub is None else pl.ds(sub * 1024, 1024)]

    arrived(p_partner)

    row_id = lax.broadcasted_iota(jnp.int32, (REQ_LEN, 256), 0)
    col_id = lax.broadcasted_iota(jnp.int32, (REQ_LEN, 256), 1)
    in_node = lax.rem(col_id, NODE_LEN)
    piece = col_id // NODE_LEN
    for r in range(2):
        leaf = leaf_ref[r]
        tenant = parent_ref[leaf]
        root = parent_ref[tenant]
        nodes = (leaf, tenant, root)
        limit = jnp.where(
            piece == 0, length_ref[leaf],
            jnp.where(piece == 1, length_ref[tenant],
                      jnp.where(piece == 2, length_ref[root], row_id + 1)),
        )
        allowed = in_node < limit

        def rows_of(i, own):
            parts = [
                kvbuf[i, n // 8, lax.rem(n // 4, 2), lax.rem(n, 4)].reshape(NODE_LEN, 512)
                for n in nodes
            ]
            return jnp.concatenate(parts + [own[r * REQ_LEN:(r + 1) * REQ_LEN]], axis=0)

        keys = rows_of(0, k_ref)
        values = rows_of(1, v_ref)
        for h in range(4):
            cols = slice(h * HEAD_DIM, (h + 1) * HEAD_DIM)
            qh = q_ref[r * REQ_LEN:(r + 1) * REQ_LEN, cols]
            scores = lax.dot_general(
                qh, keys[:, cols], (((1,), (1,)), ((), ())), preferred_element_type=F32
            ) * (1.0 / math.sqrt(HEAD_DIM))
            top = jnp.max(jnp.where(allowed, scores, -1e30), axis=-1, keepdims=True)
            weights = jnp.where(allowed, jnp.exp(scores - top), 0.0)
            total = jnp.sum(weights, axis=-1, keepdims=True)
            summed = dot(weights.astype(BF), values[:, cols])
            attn[r * REQ_LEN:(r + 1) * REQ_LEN, cols] = (summed / total).astype(BF)

    arrived(w_partner)
    for i in range(16):
        part = dot(attn[...], wbuf[i // 4, i % 4]).astype(BF)
        psend[:, :, i * 128:(i + 1) * 128] = part.reshape(4, 32, 128)
    proj_copies = [
        remote(psend.at[i], precv.at[t], peer) for i, peer in zip(tensor_ids, tensor_peers)
    ]
    down_first = [
        remote(dn_ref.at[half_rows], dnbuf.at[t, half_rows], z_neighbour(k)) for k in (1, -1)
    ]
    up_second, up_across = pass_on(up_first, up_view)
    for copy in own_small:
        copy.wait()
    arrived(small_copies)
    arrived(proj_copies)

    square = jnp.zeros((32, 1), F32)
    for j in range(4):
        cols = slice(j * 512, (j + 1) * 512)
        total = psend[t, :, cols].astype(F32)
        for i in tensor_ids:
            total = total + precv[i, :, cols].astype(F32)
        total = total + hbuf[j].astype(F32)
        resid[:, cols] = total
        square = square + jnp.sum(total * total, axis=1, keepdims=True)
    factor = lax.rsqrt(square / D + 1e-05)
    for j in range(4):
        cols = slice(j * 512, (j + 1) * 512)
        normed = (resid[:, cols] * factor * gbuf[j]).astype(BF)
        for h in (0, 1):
            xbuf[h, firsts[h], seconds[h], :, cols] = normed[h * 16:(h + 1) * 16]

    near_to, far_to = (x_neighbour, y_neighbour), (y_neighbour, x_neighbour)
    col_parts = (pl.ds(0, 1152), pl.ds(1152, 1024))

    def spread(o1, o2, to):
        copies = []
        for h in (0, 1):
            slot = xbuf.at[h, wrap(firsts[h] + o1, 4), wrap(seconds[h] + o2, 4)]
            copies += [remote(slot, slot, to[h](step)) for step in (1, -1)]
        return copies

    def relay(near, o1, o2, to):
        copies = []
        for sub, step in ((0, 1), (1, -1)):
            for h in (0, 1):
                a1 = wrap(firsts[h] + (-step if near else o1), 4)
                a2 = wrap(seconds[h] + (o2 if near else -step), 4)
                slot = xbuf.at[h, a1, a2, ALL, col_parts[sub]]
                copies.append(remote(slot, slot, to[h](step)))
        return copies

    near_first = spread(0, 0, near_to)
    far_first = {0: spread(0, 0, far_to)}
    far_second = {}
    arrived(near_first)
    near_second = relay(True, None, 0, near_to)
    far_first[3] = spread(-1, 0, far_to)
    far_first[1] = spread(1, 0, far_to)
    arrived(far_first[0])
    far_second[0] = relay(False, 0, None, far_to)
    arrived(near_second)
    far_first[2] = spread(2, 0, far_to)
    arrived(far_first[3])
    far_second[3] = relay(False, 3, None, far_to)
    arrived(far_first[1])
    far_second[1] = relay(False, 1, None, far_to)
    arrived(far_first[2])
    far_second[2] = relay(False, 2, None, far_to)
    down_second, down_across = pass_on(down_first, down_view)
    for copy in own_weights:
        copy.wait()
    arrived(up_across)

    def fill(b):
        for i, o in enumerate((b, 3 - b)):
            for h in (0, 1):
                at = i * 128 + h * 64
                rows = xbuf[h, wrap(firsts[h] + o, 4)]
                xrow[b, at:at + 64] = rows.reshape(64, D + 128)

    def hidden_units(slot, b):
        tokens = xrow[b, :, 0:D]
        gate = dot(tokens, gubuf[slot, 0])
        up = dot(tokens, gubuf[slot, 1])
        return (gate * jax.nn.sigmoid(gate) * up).astype(BF)

    def three_quarters(b):
        def step(j, c):
            slot = wrap(t + j + j // 2, 4)
            hidden = hidden_units(slot, b)
            for n in range(4):
                cols = slice(n * 512, (n + 1) * 512)
                acc[b, :, cols] += dot(hidden, dnbuf[slot, :, cols])
            return c

        lax.fori_loop(0, 3, step, 0)

    def last_quarter(b):
        lanes = lax.broadcasted_iota(jnp.int32, (256, 128), 1)
        parts = xrow[b, :, D:].astype(F32)
        route = jnp.sum(jnp.where(lax.rem(lanes, 16) == e, parts, 0.0), axis=1, keepdims=True)
        hidden = hidden_units(opposite, b)
        for n in range(4):
            cols = slice(n * 512, (n + 1) * 512)
            whole = (acc[b, :, cols] + dot(hidden, dnbuf[opposite, :, cols])) * route
            for i, o in enumerate((b, 3 - b)):
                for h in (0, 1):
                    at = i * 128 + h * 64
                    obuf[h, wrap(firsts[h] + o, 4), :, :, cols] = (
                        whole[at:at + 64].astype(BF).reshape(4, 16, 512)
                    )

    opposite = wrap(t + 2, 4)
    last_across = []
    arrived(far_second[0])
    arrived(far_second[3])
    fill(0)
    arrived(down_across)
    three_quarters(0)
    arrived(up_second)
    last_across.append(remote(up_view(opposite, None), up_view(opposite, None), partner))
    arrived(far_second[1])
    arrived(far_second[2])
    fill(1)
    three_quarters(1)
    arrived(down_second)
    last_across.append(remote(down_view(opposite, None), down_view(opposite, None), partner))
    arrived(last_across)
    last_quarter(1)

    col_halves = (slice(0, 1024), slice(1024, 2048))

    def exchange(to, at, rs_half, rs_full, h):
        def go(phase, pending):
            arrived(pending)
            if phase == 0:
                return [
                    remote(at(2, col_halves[i]), rs_half.at[h, i], to(step))
                    for i, step in ((0, 1), (1, -1))
                ]
            for i, step in ((0, 1), (1, -1)):
                ref = at(step, col_halves[i])
                ref[...] = (ref[...].astype(F32) + rs_half[h, i].astype(F32)).astype(BF)
            return [
                remote(at(step, ALL), rs_full.at[h, i], to(step))
                for i, step in ((0, 1), (1, -1))
            ]

        return go

    rows_of_half = (slice(0, 16), slice(16, 32))

    def far_at(h):
        def at(step, cols):
            return obuf.at[h, wrap(firsts[h] + step, 4), ALL, ALL, cols]

        return at

    def near_at(h):
        def at(step, cols):
            return row_sum.at[h, wrap(seconds[h] + step, 4), ALL, cols]

        return at

    far = [exchange(near_to[h], far_at(h), far_near, far_sum, h) for h in (0, 1)]
    near = [exchange(far_to[h], near_at(h), near_half, near_sum, h) for h in (0, 1)]
    pending = [far[h](0, []) for h in (0, 1)]
    last_quarter(0)
    pending = [far[h](1, pending[h]) for h in (0, 1)]
    after = []
    for h in (0, 1):
        arrived(pending[h])
        total = far_at(h)(0, ALL)[...].astype(F32)
        total = total + far_sum[h, 0].astype(F32) + far_sum[h, 1].astype(F32)
        row_sum[h] = total.astype(BF)
        after.append(near[h](0, []))
    after = [near[h](1, after[h]) for h in (0, 1)]
    for h in (0, 1):
        arrived(after[h])
        for j in range(4):
            cols = slice(j * 512, (j + 1) * 512)
            total = resid[rows_of_half[h], cols] + near_at(h)(0, cols)[...].astype(F32)
            total = total + near_sum[h, 0, :, cols].astype(F32) + near_sum[h, 1, :, cols].astype(F32)
            fin[j, rows_of_half[h]] = total.astype(BF)
    out_copies = [
        remote(fin.at[i], out_ref.at[own_rows], peer) for i, peer in zip(tensor_ids, tensor_peers)
    ]
    last = local(fin.at[t], out_ref.at[own_rows])
    last.wait()
    arrived(out_copies)
    for copy in sent:
        copy.wait_send()


def body(
    hidden_in, queries, new_keys, new_values, prefix_keys, prefix_values, node_length, parent,
    leaf_of_request, out_weight, norm_gain, expert_ids, gate_weights, gate_up, down_weight,
):
    smem = pl.BlockSpec(memory_space=pltpu.SMEM)
    vmem = pl.BlockSpec(memory_space=pltpu.VMEM)
    hbm = pl.BlockSpec(memory_space=pl.ANY)
    return pl.pallas_call(
        kernel,
        out_shape=jax.ShapeDtypeStruct(hidden_in.shape, BF),
        in_specs=[smem] * 3 + [vmem] * 7 + [hbm] * 5,
        out_specs=vmem,
        scratch_shapes=[
            pltpu.VMEM((2, 4, 2, 4, 4, 16, 512), BF),
            pltpu.VMEM((4, 4, 512, 128), BF),
            pltpu.VMEM((4, 2, 2048, 256), BF),
            pltpu.VMEM((4, 256, 2048), BF),
            pltpu.VMEM((4, 32, 512), BF),
            pltpu.VMEM((4, 1, 512), F32),
            pltpu.VMEM((4, 32, 2048), BF),
            pltpu.VMEM((4, 32, 2048), BF),
            pltpu.VMEM((32, 2048), F32),
            pltpu.VMEM((2, 4, 4, 16, 2176), BF),
            pltpu.VMEM((2, 256, 2176), BF),
            pltpu.VMEM((2, 256, 2048), F32),
            pltpu.VMEM((2, 4, 4, 16, 2048), BF),
            pltpu.VMEM((4, 32, 512), BF),
            pltpu.VMEM((128, 512), BF),
            pltpu.VMEM((2, 128, 8), F32),
            pltpu.VMEM((2, 2, 4, 16, 1024), BF),
            pltpu.VMEM((2, 2, 4, 16, 2048), BF),
            pltpu.VMEM((2, 2, 16, 1024), BF),
            pltpu.VMEM((2, 2, 16, 2048), BF),
            pltpu.VMEM((2, 4, 16, 2048), BF),
            pltpu.SemaphoreType.DMA((192,)),
            pltpu.SemaphoreType.DMA((192,)),
            pltpu.SemaphoreType.DMA((16,)),
        ],
        compiler_params=pltpu.CompilerParams(
            collective_id=0, has_side_effects=True, vmem_limit_bytes=56 << 20
        ),
        name="layer",
    )(
        leaf_of_request, parent, node_length, expert_ids.T, gate_weights.T, queries, new_keys,
        new_values, hidden_in, norm_gain[None, :], prefix_keys, prefix_values, out_weight, gate_up[0],
        down_weight[0],
    )


def solution(mesh):
    rows = P(("dp", "expert"), "tensor")
    placed = (
        rows, rows, rows, rows,
        P("dp", "tensor"),
        P("dp", "tensor"),
        P(), P(),
        P(("dp", "expert")),
        P("tensor", "expert"),
        P("tensor"),
        P(("dp", "expert"), None),
        P(("dp", "expert"), None),
        P("expert", None, None, "tensor"),
        P("expert", "tensor", None),
    )
    return jax.shard_map(body, mesh=mesh, in_specs=placed, out_specs=rows, check_vma=False)
```

```python
import math

import jax
import jax.numpy as jnp
from jax import lax
from jax.experimental import pallas as pl
from jax.experimental.pallas import tpu as pltpu
from jax.sharding import PartitionSpec as P

MESH = pl.DeviceIdType.MESH
D = 2048
HEAD_DIM = 128
REQ_LEN = 64
NODE_LEN = 64
ALL = slice(None)
BF = jnp.bfloat16
F32 = jnp.float32


def dot(a, b):
    return jnp.dot(a, b, preferred_element_type=F32)


def wrap(v, n):
    return lax.rem(v + 4 * n, n)


def kernel(
    leaf_ref, parent_ref, length_ref,
    ids_ref, gate_ref, q_ref, k_ref, v_ref, hidden_ref, gain_ref,
    pk_ref, pv_ref, w_ref, gu_ref, dn_ref,
    out_ref,
    kvbuf, wbuf, gubuf, dnbuf, gbuf, psend, precv, resid, xbuf, xrow, acc,
    obuf, fin, attn, routes, far_near, far_sum, near_half, near_sum, row_sum, last_hidden,
    send_sems, recv_sems, local_sems, out_sems,
):
    dp = lax.axis_index("dp")
    e = lax.axis_index("expert")
    t = lax.axis_index("tensor")
    zh, core = dp // 2, lax.rem(dp, 2)
    x, y = e // 4, lax.rem(e, 4)
    z = zh * 4 + t

    def dev(dp_, e_, t_):
        return {"dp": dp_, "expert": e_, "tensor": t_}

    def z_neighbour(step):
        zz = wrap(z + step, 16)
        return dev((zz // 4) * 2 + core, e, lax.rem(zz, 4))

    def x_neighbour(step):
        return dev(dp, wrap(x + step, 4) * 4 + y, t)

    def y_neighbour(step):
        return dev(dp, x * 4 + wrap(y + step, 4), t)

    partner = dev(zh * 2 + (1 - core), e, t)
    tensor_ids = [wrap(t + k, 4) for k in (1, 2, 3)]
    tensor_peers = [dev(dp, e, i) for i in tensor_ids]

    def z_hi_neighbour(step):
        return dev(wrap(zh + step, 4) * 2 + core, e, t)

    barrier = pltpu.get_barrier_semaphore()
    greeted = [partner] + tensor_peers
    for to in (x_neighbour, y_neighbour, z_neighbour, z_hi_neighbour):
        greeted += [to(1), to(-1)]
    for peer in greeted:
        pl.semaphore_signal(barrier, inc=1, device_id=peer, device_id_type=MESH)

    counts = [0, 0]
    sent = []

    def local(src, dst):
        copy = pltpu.make_async_copy(src, dst, local_sems.at[counts[1]])
        counts[1] += 1
        copy.start()
        return copy

    def remote(src, dst, peer):
        i = counts[0]
        counts[0] += 1
        copy = pltpu.make_async_remote_copy(
            src_ref=src, dst_ref=dst, send_sem=send_sems.at[i], recv_sem=recv_sems.at[i],
            device_id=peer, device_id_type=MESH,
        )
        copy.start()
        sent.append(copy)
        return copy

    def arrived(copies):
        for copy in copies:
            copy.wait_recv()

    def ag_first(view, phase):
        copies = []
        for h in (0, 1):
            p1, p2 = (x, y) if h == 0 else (y, x)
            to = (x_neighbour, y_neighbour)[(h + phase) % 2]
            own = view(h, p1, p2, None) if phase == 0 else view(h, ALL, p2, None)
            for step in (1, -1):
                copies.append(remote(own, own, to(step)))
        return copies

    def ag_second(view, phase):
        copies = []
        for h in (0, 1):
            p1, p2 = (x, y) if h == 0 else (y, x)
            to = (x_neighbour, y_neighbour)[(h + phase) % 2]
            for sub, step in ((0, 1), (1, -1)):
                if phase == 0:
                    slot = view(h, wrap(p1 - step, 4), p2, sub)
                else:
                    slot = view(h, ALL, wrap(p2 - step, 4), sub)
                copies.append(remote(slot, slot, to(step)))
        return copies

    def w_view(h, a1, a2, sub):
        xi, yi = (a1, a2) if h == 0 else (a2, a1)
        start = core * 256 + h * 128
        rows = pl.ds(start, 128) if sub is None else pl.ds(start + sub * 64, 64)
        return wbuf.at[xi, yi, rows]

    def kv_view(zs):
        def view(h, a1, a2, sub):
            xi, yi = (a1, a2) if h == 0 else (a2, a1)
            cols = ALL if sub is None else pl.ds(sub * 256, 256)
            return kvbuf.at[h, zs, core, xi, yi, ALL, cols]

        return view

    def gather(view, done):
        for phase in (0, 1):
            copies = ag_first(view, phase)
            yield
            arrived(copies)
            copies = ag_second(view, phase)
            yield
            arrived(copies)
        done()
        yield

    rows16 = pl.ds(pl.multiple_of(e * 16, 16), 16)
    w_rows = pl.ds(pl.multiple_of(core * 256, 256), 256)
    own_w = local(w_ref.at[w_rows], wbuf.at[x, y, w_rows])
    own_kv = [
        local(pk_ref.at[rows16], kvbuf.at[0, zh, core, x, y]),
        local(pv_ref.at[rows16], kvbuf.at[1, zh, core, x, y]),
    ]
    own_rows = pl.ds(pl.multiple_of(t * 32, 32), 32)
    own_gain = local(gain_ref, gbuf.at[t])
    own_weights = [local(gu_ref, gubuf.at[t]), local(dn_ref, dnbuf.at[t])]

    routes[0] = ids_ref[...].astype(F32).T
    routes[1] = gate_ref[...].T
    named, gates = routes[0, own_rows], routes[1, own_rows]
    lane = lax.broadcasted_iota(jnp.int32, (32, 128), 1)
    lane_expert = jnp.where(lane < 48, lax.rem(lane, 16), -1).astype(F32)
    weight = jnp.zeros((32, 128), F32)
    for i in range(8):
        weight = weight + jnp.where(lane_expert == named[:, i:i + 1], gates[:, i:i + 1], 0.0)
    high = weight.astype(BF)
    rest = weight - high.astype(F32)
    middle = rest.astype(BF)
    low = (rest - middle.astype(F32)).astype(BF)
    routed = jnp.where(lane < 16, high, jnp.where(lane < 32, middle, low))
    firsts, seconds = (x, y), (y, x)
    for h in (0, 1):
        xbuf[h, firsts[h], seconds[h], :, D:] = routed[h * 16:(h + 1) * 16]
    acc[...] = jnp.zeros_like(acc)

    pl.semaphore_wait(barrier, len(greeted))

    z_copies = []
    for step in (1, -1):
        for i, ref in ((0, pk_ref), (1, pv_ref)):
            z_copies.append(
                remote(ref.at[rows16], kvbuf.at[i, zh, core, x, y], z_hi_neighbour(step))
            )
    for copy in own_kv:
        copy.wait()
    p_partner, w_partner = [], []

    def prefix_gather(zs):
        def done():
            for i in (0, 1):
                piece = kvbuf.at[i, zs, core]
                p_partner.append(remote(piece, piece, partner))

        return gather(kv_view(zs), done)

    def w_done():
        rows = wbuf.at[:, :, w_rows]
        w_partner.append(remote(rows, rows, partner))

    mine, w_all = prefix_gather(zh), gather(w_view, w_done)
    next(mine)
    own_w.wait()
    next(w_all)
    half_rows = pl.ds(pl.multiple_of(core * 128, 128), 128)

    def up_rows(start, size):
        rows = pl.ds(start, size)
        return [
            remote(gu_ref.at[core, rows], gubuf.at[t, core, rows], z_neighbour(k)) for k in (1, -1)
        ]

    up_first = up_rows(0, 256)

    next(mine)
    next(w_all)
    arrived(z_copies)
    z_copies = []
    for i, step in ((0, 1), (1, -1)):
        slot = kvbuf.at[i, wrap(zh - step, 4), core, x, y]
        z_copies.append(remote(slot, slot, z_hi_neighbour(step)))
    up_first += up_rows(256, 1792)

    def down_rows(start):
        rows = pl.ds(pl.multiple_of(core * 128 + start, 64), 64)
        return [remote(dn_ref.at[rows], dnbuf.at[t, rows], z_neighbour(k)) for k in (1, -1)]

    down_first = down_rows(0)
    small_copies = [remote(gain_ref, gbuf.at[t], peer) for peer in tensor_peers]
    before, behind = prefix_gather(wrap(zh - 1, 4)), prefix_gather(wrap(zh + 1, 4))
    next(before)
    next(behind)
    next(mine)
    next(w_all)
    next(before)
    next(behind)
    next(mine)
    arrived(z_copies)
    across = prefix_gather(wrap(zh + 2, 4))
    next(across)
    next(w_all)
    next(before)
    next(behind)
    next(mine)
    next(across)
    next(before)
    next(behind)
    next(w_all)
    next(across)
    next(before)
    next(behind)
    next(across)
    next(across)

    def pass_on(arrivals, views):
        arrived(arrivals)
        on, across = [], []
        for sub, step in ((0, 1), (1, -1)):
            slot = wrap(t - step, 4)
            part = views(slot, sub)
            on.append(remote(part, part, z_neighbour(step)))
            whole = views(slot, None)
            across.append(remote(whole, whole, partner))
        return on, across

    def up_view(slot, sub):
        return gubuf.at[slot, core, ALL if sub is None else pl.ds(sub * 1024, 1024)]

    def down_view(slot, sub):
        return dnbuf.at[slot, half_rows, ALL if sub is None else pl.ds(sub * 1024, 1024)]

    arrived(p_partner)

    row_id = lax.broadcasted_iota(jnp.int32, (REQ_LEN, 256), 0)
    col_id = lax.broadcasted_iota(jnp.int32, (REQ_LEN, 256), 1)
    in_node = lax.rem(col_id, NODE_LEN)
    piece = col_id // NODE_LEN
    for r in range(2):
        leaf = leaf_ref[r]
        tenant = parent_ref[leaf]
        root = parent_ref[tenant]
        nodes = (leaf, tenant, root)
        limit = jnp.where(
            piece == 0, length_ref[leaf],
            jnp.where(piece == 1, length_ref[tenant],
                      jnp.where(piece == 2, length_ref[root], row_id + 1)),
        )
        allowed = in_node < limit

        def rows_of(i, own):
            parts = [
                kvbuf[i, n // 8, lax.rem(n // 4, 2), lax.rem(n, 4)].reshape(NODE_LEN, 512)
                for n in nodes
            ]
            return jnp.concatenate(parts + [own[r * REQ_LEN:(r + 1) * REQ_LEN]], axis=0)

        keys = rows_of(0, k_ref)
        values = rows_of(1, v_ref)
        for h in range(4):
            cols = slice(h * HEAD_DIM, (h + 1) * HEAD_DIM)
            qh = q_ref[r * REQ_LEN:(r + 1) * REQ_LEN, cols]
            scores = lax.dot_general(
                qh, keys[:, cols], (((1,), (1,)), ((), ())), preferred_element_type=F32
            ) * (1.0 / math.sqrt(HEAD_DIM))
            top = jnp.max(jnp.where(allowed, scores, -1e30), axis=-1, keepdims=True)
            weights = jnp.where(allowed, jnp.exp(scores - top), 0.0)
            total = jnp.sum(weights, axis=-1, keepdims=True)
            summed = dot(weights.astype(BF), values[:, cols])
            attn[r * REQ_LEN:(r + 1) * REQ_LEN, cols] = (summed / total).astype(BF)

    arrived(w_partner)
    for i in range(16):
        part = dot(attn[...], wbuf[i // 4, i % 4])
        mine_too = (t == i // 4).astype(F32)
        part = part + mine_too * hidden_ref[:, (i % 4) * 128:(i % 4 + 1) * 128].astype(F32)
        psend[:, :, i * 128:(i + 1) * 128] = part.astype(BF).reshape(4, 32, 128)
    proj_copies = [
        remote(psend.at[i], precv.at[t], peer) for i, peer in zip(tensor_ids, tensor_peers)
    ]
    down_first += down_rows(64)
    up_second, up_across = pass_on(up_first, up_view)
    own_gain.wait()
    arrived(small_copies)
    arrived(proj_copies)

    square = jnp.zeros((32, 1), F32)
    for j in range(4):
        cols = slice(j * 512, (j + 1) * 512)
        total = psend[t, :, cols].astype(F32)
        for i in tensor_ids:
            total = total + precv[i, :, cols].astype(F32)
        resid[:, cols] = total
        square = square + jnp.sum(total * total, axis=1, keepdims=True)
    factor = lax.rsqrt(square / D + 1e-05)
    for j in range(4):
        cols = slice(j * 512, (j + 1) * 512)
        normed = (resid[:, cols] * factor * gbuf[j]).astype(BF)
        for h in (0, 1):
            xbuf[h, firsts[h], seconds[h], :, cols] = normed[h * 16:(h + 1) * 16]

    near_to, far_to = (x_neighbour, y_neighbour), (y_neighbour, x_neighbour)
    col_parts = (pl.ds(0, 1152), pl.ds(1152, 1024))

    def spread(o1, o2, to):
        copies = []
        for h in (0, 1):
            slot = xbuf.at[h, wrap(firsts[h] + o1, 4), wrap(seconds[h] + o2, 4)]
            copies += [remote(slot, slot, to[h](step)) for step in (1, -1)]
        return copies

    def relay(near, o1, o2, to):
        copies = []
        for sub, step in ((0, 1), (1, -1)):
            for h in (0, 1):
                a1 = wrap(firsts[h] + (-step if near else o1), 4)
                a2 = wrap(seconds[h] + (o2 if near else -step), 4)
                slot = xbuf.at[h, a1, a2, ALL, col_parts[sub]]
                copies.append(remote(slot, slot, to[h](step)))
        return copies

    near_first = spread(0, 0, near_to)
    far_first = {0: spread(0, 0, far_to)}
    far_second = {}
    arrived(near_first)
    near_second = relay(True, None, 0, near_to)
    far_first[3] = spread(-1, 0, far_to)
    far_first[1] = spread(1, 0, far_to)
    arrived(far_first[0])
    far_second[0] = relay(False, 0, None, far_to)
    arrived(near_second)
    far_first[2] = spread(2, 0, far_to)
    down_second, down_across = pass_on(down_first, down_view)
    arrived(far_first[3])
    far_second[3] = relay(False, 3, None, far_to)
    arrived(far_first[1])
    far_second[1] = relay(False, 1, None, far_to)
    arrived(far_first[2])
    far_second[2] = relay(False, 2, None, far_to)
    for copy in own_weights:
        copy.wait()
    arrived(up_across)

    def fill(b):
        for i, o in enumerate((b, 3 - b)):
            for h in (0, 1):
                at = i * 128 + h * 64
                rows = xbuf[h, wrap(firsts[h] + o, 4)]
                xrow[b, at:at + 64] = rows.reshape(64, D + 128)

    def hidden_units(slot, b):
        tokens = xrow[b, :, 0:D]
        gate = dot(tokens, gubuf[slot, 0])
        up = dot(tokens, gubuf[slot, 1])
        return (gate * jax.nn.sigmoid(gate) * up).astype(BF)

    def three_quarters(b):
        def step(j, c):
            slot = wrap(t + j + j // 2, 4)
            hidden = hidden_units(slot, b)
            for n in range(4):
                cols = slice(n * 512, (n + 1) * 512)
                acc[b, :, cols] += dot(hidden, dnbuf[slot, :, cols])
            return c

        lax.fori_loop(0, 3, step, 0)

    def routes_of(b):
        lanes = lax.broadcasted_iota(jnp.int32, (256, 128), 1)
        parts = xrow[b, :, D:].astype(F32)
        return jnp.sum(jnp.where(lax.rem(lanes, 16) == e, parts, 0.0), axis=1, keepdims=True)

    def last_down(b, c):
        for n in (2 * c, 2 * c + 1):
            cols = slice(n * 512, (n + 1) * 512)
            whole = (acc[b, :, cols] + dot(last_hidden[b], dnbuf[opposite, :, cols])) * route[b]
            for i, o in enumerate((b, 3 - b)):
                for h in (0, 1):
                    at = i * 128 + h * 64
                    obuf[h, wrap(firsts[h] + o, 4), :, :, cols] = (
                        whole[at:at + 64].astype(BF).reshape(4, 16, 512)
                    )

    opposite = wrap(t + 2, 4)
    arrived(far_second[0])
    arrived(far_second[3])
    fill(0)
    arrived(down_across)
    three_quarters(0)
    arrived(up_second)
    up_across = remote(up_view(opposite, None), up_view(opposite, None), partner)
    arrived(far_second[1])
    arrived(far_second[2])
    fill(1)
    three_quarters(1)
    arrived([up_across])
    route = [routes_of(b) for b in (0, 1)]
    for b in (0, 1):
        last_hidden[b] = hidden_units(opposite, b)
    arrived(down_second)
    down_across = remote(down_view(opposite, None), down_view(opposite, None), partner)
    arrived([down_across])

    both = ((0, 1), (1, -1))

    def far_at(h):
        def at(step, cols):
            return obuf.at[h, wrap(firsts[h] + step, 4), ALL, ALL, cols]

        return at

    def near_at(h):
        def at(step, cols):
            return row_sum.at[h, wrap(seconds[h] + step, 4), ALL, cols]

        return at

    def part_of(c, i):
        return pl.ds(c * 1024 + i * 512, 512)

    def send_opposite(at, to, half, h, c):
        return [remote(at(2, part_of(c, i)), half.at[h, c, i], to[h](k)) for i, k in both]

    def send_sides(at, to, half, full, h, c, pending):
        arrived(pending)
        for i, k in both:
            ref = at(k, part_of(c, i))
            ref[...] = (ref[...].astype(F32) + half[h, c, i].astype(F32)).astype(BF)
        whole = pl.ds(c * 1024, 1024)
        return [remote(at(k, whole), full.at[h, c, i], to[h](k)) for i, k in both]

    chains = [(h, c) for c in (0, 1) for h in (0, 1)]
    flight = {}
    for c in (0, 1):
        last_down(1, c)
        for h in (0, 1):
            flight[h, c] = send_opposite(far_at(h), near_to, far_near, h, c)
    for c in (0, 1):
        last_down(0, c)
        for h in (0, 1):
            flight[h, c] = send_sides(
                far_at(h), near_to, far_near, far_sum, h, c, flight[h, c]
            )
    for h, c in chains:
        arrived(flight[h, c])
        whole = pl.ds(c * 1024, 1024)
        total = far_at(h)(0, whole)[...].astype(F32)
        total = total + far_sum[h, c, 0].astype(F32) + far_sum[h, c, 1].astype(F32)
        row_sum[h, :, :, c * 1024:(c + 1) * 1024] = total.astype(BF)
        flight[h, c] = send_opposite(near_at(h), far_to, near_half, h, c)
    for h, c in chains:
        flight[h, c] = send_sides(
            near_at(h), far_to, near_half, near_sum, h, c, flight[h, c]
        )
    def out_copy(src, rows, send, recv, peer):
        return pltpu.make_async_remote_copy(
            src_ref=src, dst_ref=out_ref.at[rows], send_sem=out_sems.at[0, send],
            recv_sem=out_sems.at[1, recv], device_id=peer, device_id_type=MESH,
        )

    for h, c in chains:
        arrived(flight[h, c])
        rows = slice(h * 16, (h + 1) * 16)
        for j in (0, 1):
            cols = slice(c * 1024 + j * 512, c * 1024 + (j + 1) * 512)
            here = slice(j * 512, (j + 1) * 512)
            total = resid[rows, cols] + near_at(h)(0, cols)[...].astype(F32)
            for i in (0, 1):
                total = total + near_sum[h, c, i, :, here].astype(F32)
            fin[2 * c + j, rows] = total.astype(BF)
        if h == 1:
            for j in (2 * c, 2 * c + 1):

                @pl.when(t != j)
                def _(j=j):
                    out_copy(fin.at[j], own_rows, j, t, dev(dp, e, j)).start()

    last = local(fin.at[t], out_ref.at[own_rows])
    last.wait()
    for i, peer in zip(tensor_ids, tensor_peers):
        from_peer = pl.ds(pl.multiple_of(i * 32, 32), 32)
        out_copy(fin.at[i], from_peer, i, i, peer).wait()
    for copy in sent:
        copy.wait_send()


def body(
    hidden_in, queries, new_keys, new_values, prefix_keys, prefix_values, node_length, parent,
    leaf_of_request, out_weight, norm_gain, expert_ids, gate_weights, gate_up, down_weight,
):
    smem = pl.BlockSpec(memory_space=pltpu.SMEM)
    vmem = pl.BlockSpec(memory_space=pltpu.VMEM)
    hbm = pl.BlockSpec(memory_space=pl.ANY)
    return pl.pallas_call(
        kernel,
        out_shape=jax.ShapeDtypeStruct(hidden_in.shape, BF),
        in_specs=[smem] * 3 + [vmem] * 7 + [hbm] * 5,
        out_specs=vmem,
        scratch_shapes=[
            pltpu.VMEM((2, 4, 2, 4, 4, 16, 512), BF),
            pltpu.VMEM((4, 4, 512, 128), BF),
            pltpu.VMEM((4, 2, 2048, 256), BF),
            pltpu.VMEM((4, 256, 2048), BF),
            pltpu.VMEM((4, 1, 512), F32),
            pltpu.VMEM((4, 32, 2048), BF),
            pltpu.VMEM((4, 32, 2048), BF),
            pltpu.VMEM((32, 2048), F32),
            pltpu.VMEM((2, 4, 4, 16, 2176), BF),
            pltpu.VMEM((2, 256, 2176), BF),
            pltpu.VMEM((2, 256, 2048), F32),
            pltpu.VMEM((2, 4, 4, 16, 2048), BF),
            pltpu.VMEM((4, 32, 512), BF),
            pltpu.VMEM((128, 512), BF),
            pltpu.VMEM((2, 128, 8), F32),
            pltpu.VMEM((2, 2, 2, 4, 16, 512), BF),
            pltpu.VMEM((2, 2, 2, 4, 16, 1024), BF),
            pltpu.VMEM((2, 2, 2, 16, 512), BF),
            pltpu.VMEM((2, 2, 2, 16, 1024), BF),
            pltpu.VMEM((2, 4, 16, 2048), BF),
            pltpu.VMEM((2, 256, 256), BF),
            pltpu.SemaphoreType.DMA((224,)),
            pltpu.SemaphoreType.DMA((224,)),
            pltpu.SemaphoreType.DMA((16,)),
            pltpu.SemaphoreType.DMA((2, 4)),
        ],
        compiler_params=pltpu.CompilerParams(
            collective_id=0, has_side_effects=True, vmem_limit_bytes=56 << 20
        ),
        name="layer",
    )(
        leaf_of_request, parent, node_length, expert_ids.T, gate_weights.T, queries, new_keys,
        new_values, hidden_in, norm_gain[None, :], prefix_keys, prefix_values, out_weight, gate_up[0],
        down_weight[0],
    )


def solution(mesh):
    rows = P(("dp", "expert"), "tensor")
    placed = (
        rows, rows, rows, rows,
        P("dp", "tensor"),
        P("dp", "tensor"),
        P(), P(),
        P(("dp", "expert")),
        P("tensor", "expert"),
        P("tensor"),
        P(("dp", "expert"), None),
        P(("dp", "expert"), None),
        P("expert", None, None, "tensor"),
        P("expert", "tensor", None),
    )
    return jax.shard_map(body, mesh=mesh, in_specs=placed, out_specs=rows, check_vma=False)
```

```python
import math

import jax
import jax.numpy as jnp
from jax import lax
from jax.experimental import pallas as pl
from jax.experimental.pallas import tpu as pltpu
from jax.sharding import PartitionSpec as P

MESH = pl.DeviceIdType.MESH
D = 2048
HEAD_DIM = 128
REQ_LEN = 64
NODE_LEN = 64
ALL = slice(None)
BF = jnp.bfloat16
F32 = jnp.float32


def dot(a, b):
    return jnp.dot(a, b, preferred_element_type=F32)


def wrap(v, n):
    return lax.rem(v + 4 * n, n)


def kernel(
    leaf_ref, parent_ref, length_ref,
    ids_in, gate_in, q_in, k_in, v_in, hidden_in, gain_ref,
    pk_ref, pv_ref, w_ref, gu_ref, dn_ref,
    out_ref,
    kvbuf, wbuf, gubuf, dnbuf, gbuf, psend, precv, resid, xbuf, xrow, acc,
    obuf, fin, attn, routes, far_near, far_sum, near_half, near_sum, row_sum, last_hidden,
    ids_ref, gate_ref, q_ref, k_ref, v_ref, hidden_ref,
    send_sems, recv_sems, local_sems, out_sems,
):
    dp = lax.axis_index("dp")
    e = lax.axis_index("expert")
    t = lax.axis_index("tensor")
    zh, core = dp // 2, lax.rem(dp, 2)
    x, y = e // 4, lax.rem(e, 4)
    z = zh * 4 + t

    def dev(dp_, e_, t_):
        return {"dp": dp_, "expert": e_, "tensor": t_}

    def z_neighbour(step):
        zz = wrap(z + step, 16)
        return dev((zz // 4) * 2 + core, e, lax.rem(zz, 4))

    def x_neighbour(step):
        return dev(dp, wrap(x + step, 4) * 4 + y, t)

    def y_neighbour(step):
        return dev(dp, x * 4 + wrap(y + step, 4), t)

    partner = dev(zh * 2 + (1 - core), e, t)
    tensor_ids = [wrap(t + k, 4) for k in (1, 2, 3)]
    tensor_peers = [dev(dp, e, i) for i in tensor_ids]

    def z_hi_neighbour(step):
        return dev(wrap(zh + step, 4) * 2 + core, e, t)

    barrier = pltpu.get_barrier_semaphore()
    greeted = [partner] + tensor_peers
    for to in (x_neighbour, y_neighbour, z_neighbour, z_hi_neighbour):
        greeted += [to(1), to(-1)]
    for peer in greeted:
        pl.semaphore_signal(barrier, inc=1, device_id=peer, device_id_type=MESH)

    counts = [0, 0]
    sent = []

    def local(src, dst):
        copy = pltpu.make_async_copy(src, dst, local_sems.at[counts[1]])
        counts[1] += 1
        copy.start()
        return copy

    def remote(src, dst, peer):
        i = counts[0]
        counts[0] += 1
        copy = pltpu.make_async_remote_copy(
            src_ref=src, dst_ref=dst, send_sem=send_sems.at[i], recv_sem=recv_sems.at[i],
            device_id=peer, device_id_type=MESH,
        )
        copy.start()
        sent.append(copy)
        return copy

    def arrived(copies):
        for copy in copies:
            copy.wait_recv()

    def ag_first(view, phase):
        copies = []
        for h in (0, 1):
            p1, p2 = (x, y) if h == 0 else (y, x)
            to = (x_neighbour, y_neighbour)[(h + phase) % 2]
            own = view(h, p1, p2, None) if phase == 0 else view(h, ALL, p2, None)
            for step in (1, -1):
                copies.append(remote(own, own, to(step)))
        return copies

    def ag_second(view, phase):
        copies = []
        for h in (0, 1):
            p1, p2 = (x, y) if h == 0 else (y, x)
            to = (x_neighbour, y_neighbour)[(h + phase) % 2]
            for sub, step in ((0, 1), (1, -1)):
                if phase == 0:
                    slot = view(h, wrap(p1 - step, 4), p2, sub)
                else:
                    slot = view(h, ALL, wrap(p2 - step, 4), sub)
                copies.append(remote(slot, slot, to(step)))
        return copies

    def w_view(h, a1, a2, sub):
        xi, yi = (a1, a2) if h == 0 else (a2, a1)
        start = core * 256 + h * 128
        rows = pl.ds(start, 128) if sub is None else pl.ds(start + sub * 64, 64)
        return wbuf.at[xi, yi, rows]

    def kv_view(zs):
        def view(h, a1, a2, sub):
            xi, yi = (a1, a2) if h == 0 else (a2, a1)
            cols = ALL if sub is None else pl.ds(sub * 256, 256)
            return kvbuf.at[h, zs, core, xi, yi, ALL, cols]

        return view

    def gather(view, done):
        for phase in (0, 1):
            copies = ag_first(view, phase)
            yield
            arrived(copies)
            copies = ag_second(view, phase)
            yield
            arrived(copies)
        done()
        yield

    rows16 = pl.ds(pl.multiple_of(e * 16, 16), 16)
    w_rows = pl.ds(pl.multiple_of(core * 256, 256), 256)
    own_w = local(w_ref.at[w_rows], wbuf.at[x, y, w_rows])
    own_kv = [
        local(pk_ref.at[rows16], kvbuf.at[0, zh, core, x, y]),
        local(pv_ref.at[rows16], kvbuf.at[1, zh, core, x, y]),
    ]
    own_rows = pl.ds(pl.multiple_of(t * 32, 32), 32)
    own_gain = local(gain_ref, gbuf.at[t])
    own_routes = [local(ids_in, ids_ref), local(gate_in, gate_ref)]
    own_inputs = [
        local(src, dst) for src, dst in (
            (q_in, q_ref), (k_in, k_ref), (v_in, v_ref), (hidden_in, hidden_ref)
        )
    ]
    own_weights = [local(gu_ref, gubuf.at[t]), local(dn_ref, dnbuf.at[t])]

    pl.semaphore_wait(barrier, len(greeted))

    z_copies = []
    for step in (1, -1):
        for i, ref in ((0, pk_ref), (1, pv_ref)):
            z_copies.append(
                remote(ref.at[rows16], kvbuf.at[i, zh, core, x, y], z_hi_neighbour(step))
            )
    for copy in own_kv:
        copy.wait()
    p_partner, w_partner = [], []

    def prefix_gather(zs):
        def done():
            for i in (0, 1):
                piece = kvbuf.at[i, zs, core]
                p_partner.append(remote(piece, piece, partner))

        return gather(kv_view(zs), done)

    def w_done():
        rows = wbuf.at[:, :, w_rows]
        w_partner.append(remote(rows, rows, partner))

    mine, w_all = prefix_gather(zh), gather(w_view, w_done)
    next(mine)
    own_w.wait()
    next(w_all)
    half_rows = pl.ds(pl.multiple_of(core * 128, 128), 128)

    def up_rows(start, size):
        rows = pl.ds(start, size)
        return [
            remote(gu_ref.at[core, rows], gubuf.at[t, core, rows], z_neighbour(k)) for k in (1, -1)
        ]

    up_first = up_rows(0, 256)

    for copy in own_routes:
        copy.wait()
    routes[0] = ids_ref[...].astype(F32).T
    routes[1] = gate_ref[...].T
    named, gates = routes[0, own_rows], routes[1, own_rows]
    lane = lax.broadcasted_iota(jnp.int32, (32, 128), 1)
    lane_expert = jnp.where(lane < 48, lax.rem(lane, 16), -1).astype(F32)
    weight = jnp.zeros((32, 128), F32)
    for i in range(8):
        weight = weight + jnp.where(lane_expert == named[:, i:i + 1], gates[:, i:i + 1], 0.0)
    high = weight.astype(BF)
    rest = weight - high.astype(F32)
    middle = rest.astype(BF)
    low = (rest - middle.astype(F32)).astype(BF)
    routed = jnp.where(lane < 16, high, jnp.where(lane < 32, middle, low))
    firsts, seconds = (x, y), (y, x)
    for h in (0, 1):
        xbuf[h, firsts[h], seconds[h], :, D:] = routed[h * 16:(h + 1) * 16]
    acc[...] = jnp.zeros_like(acc)


    next(mine)
    next(w_all)
    arrived(z_copies)
    z_copies = []
    for i, step in ((0, 1), (1, -1)):
        slot = kvbuf.at[i, wrap(zh - step, 4), core, x, y]
        z_copies.append(remote(slot, slot, z_hi_neighbour(step)))
    up_first += up_rows(256, 1792)

    def down_rows(start):
        rows = pl.ds(pl.multiple_of(core * 128 + start, 64), 64)
        return [remote(dn_ref.at[rows], dnbuf.at[t, rows], z_neighbour(k)) for k in (1, -1)]

    down_first = down_rows(0)
    small_copies = [remote(gain_ref, gbuf.at[t], peer) for peer in tensor_peers]
    before, behind = prefix_gather(wrap(zh - 1, 4)), prefix_gather(wrap(zh + 1, 4))
    next(before)
    next(behind)
    next(mine)
    next(w_all)
    next(before)
    next(behind)
    next(mine)
    arrived(z_copies)
    across = prefix_gather(wrap(zh + 2, 4))
    next(across)
    next(w_all)
    next(before)
    next(behind)
    next(mine)
    next(across)
    next(before)
    next(behind)
    next(w_all)
    next(across)
    next(before)
    next(behind)
    next(across)
    next(across)

    def pass_on(arrivals, views):
        arrived(arrivals)
        on, across = [], []
        for sub, step in ((0, 1), (1, -1)):
            slot = wrap(t - step, 4)
            part = views(slot, sub)
            on.append(remote(part, part, z_neighbour(step)))
            whole = views(slot, None)
            across.append(remote(whole, whole, partner))
        return on, across

    def up_view(slot, sub):
        return gubuf.at[slot, core, ALL if sub is None else pl.ds(sub * 1024, 1024)]

    def down_view(slot, sub):
        return dnbuf.at[slot, half_rows, ALL if sub is None else pl.ds(sub * 1024, 1024)]

    for copy in own_inputs:
        copy.wait()
    arrived(p_partner)

    row_id = lax.broadcasted_iota(jnp.int32, (REQ_LEN, 256), 0)
    col_id = lax.broadcasted_iota(jnp.int32, (REQ_LEN, 256), 1)
    in_node = lax.rem(col_id, NODE_LEN)
    piece = col_id // NODE_LEN
    for r in range(2):
        leaf = leaf_ref[r]
        tenant = parent_ref[leaf]
        root = parent_ref[tenant]
        nodes = (leaf, tenant, root)
        limit = jnp.where(
            piece == 0, length_ref[leaf],
            jnp.where(piece == 1, length_ref[tenant],
                      jnp.where(piece == 2, length_ref[root], row_id + 1)),
        )
        allowed = in_node < limit

        def rows_of(i, own):
            parts = [
                kvbuf[i, n // 8, lax.rem(n // 4, 2), lax.rem(n, 4)].reshape(NODE_LEN, 512)
                for n in nodes
            ]
            return jnp.concatenate(parts + [own[r * REQ_LEN:(r + 1) * REQ_LEN]], axis=0)

        keys = rows_of(0, k_ref)
        values = rows_of(1, v_ref)
        for h in range(4):
            cols = slice(h * HEAD_DIM, (h + 1) * HEAD_DIM)
            qh = q_ref[r * REQ_LEN:(r + 1) * REQ_LEN, cols]
            scores = lax.dot_general(
                qh, keys[:, cols], (((1,), (1,)), ((), ())), preferred_element_type=F32
            ) * (1.0 / math.sqrt(HEAD_DIM))
            top = jnp.max(jnp.where(allowed, scores, -1e30), axis=-1, keepdims=True)
            weights = jnp.where(allowed, jnp.exp(scores - top), 0.0)
            total = jnp.sum(weights, axis=-1, keepdims=True)
            summed = dot(weights.astype(BF), values[:, cols])
            attn[r * REQ_LEN:(r + 1) * REQ_LEN, cols] = (summed / total).astype(BF)

    arrived(w_partner)
    for i in range(16):
        part = dot(attn[...], wbuf[i // 4, i % 4])
        mine_too = (t == i // 4).astype(F32)
        part = part + mine_too * hidden_ref[:, (i % 4) * 128:(i % 4 + 1) * 128].astype(F32)
        psend[:, :, i * 128:(i + 1) * 128] = part.astype(BF).reshape(4, 32, 128)
    proj_copies = [
        remote(psend.at[i], precv.at[t], peer) for i, peer in zip(tensor_ids, tensor_peers)
    ]
    down_first += down_rows(64)
    own_gain.wait()
    arrived(small_copies)
    arrived(proj_copies)
    up_second, up_across = pass_on(up_first, up_view)

    square = jnp.zeros((32, 1), F32)
    for j in range(4):
        cols = slice(j * 512, (j + 1) * 512)
        total = psend[t, :, cols].astype(F32)
        for i in tensor_ids:
            total = total + precv[i, :, cols].astype(F32)
        resid[:, cols] = total
        square = square + jnp.sum(total * total, axis=1, keepdims=True)
    factor = lax.rsqrt(square / D + 1e-05)
    for j in range(4):
        cols = slice(j * 512, (j + 1) * 512)
        normed = (resid[:, cols] * factor * gbuf[j]).astype(BF)
        for h in (0, 1):
            xbuf[h, firsts[h], seconds[h], :, cols] = normed[h * 16:(h + 1) * 16]

    near_to, far_to = (x_neighbour, y_neighbour), (y_neighbour, x_neighbour)
    col_parts = (pl.ds(0, 1152), pl.ds(1152, 1024))

    def spread(o1, o2, to):
        copies = []
        for h in (0, 1):
            slot = xbuf.at[h, wrap(firsts[h] + o1, 4), wrap(seconds[h] + o2, 4)]
            copies += [remote(slot, slot, to[h](step)) for step in (1, -1)]
        return copies

    def relay(near, o1, o2, to):
        copies = []
        for sub, step in ((0, 1), (1, -1)):
            for h in (0, 1):
                a1 = wrap(firsts[h] + (-step if near else o1), 4)
                a2 = wrap(seconds[h] + (o2 if near else -step), 4)
                slot = xbuf.at[h, a1, a2, ALL, col_parts[sub]]
                copies.append(remote(slot, slot, to[h](step)))
        return copies

    near_first = spread(0, 0, near_to)
    far_first = {0: spread(0, 0, far_to)}
    far_second = {}
    arrived(near_first)
    near_second = relay(True, None, 0, near_to)
    far_first[3] = spread(-1, 0, far_to)
    far_first[1] = spread(1, 0, far_to)
    arrived(far_first[0])
    far_second[0] = relay(False, 0, None, far_to)
    arrived(near_second)
    far_first[2] = spread(2, 0, far_to)
    down_second, down_across = pass_on(down_first, down_view)
    arrived(far_first[3])
    far_second[3] = relay(False, 3, None, far_to)
    arrived(far_first[1])
    far_second[1] = relay(False, 1, None, far_to)
    arrived(far_first[2])
    far_second[2] = relay(False, 2, None, far_to)
    for copy in own_weights:
        copy.wait()
    arrived(up_across)

    def fill(b):
        for i, o in enumerate((b, 3 - b)):
            for h in (0, 1):
                at = i * 128 + h * 64
                rows = xbuf[h, wrap(firsts[h] + o, 4)]
                xrow[b, at:at + 64] = rows.reshape(64, D + 128)

    def hidden_units(slot, b):
        tokens = xrow[b, :, 0:D]
        gate = dot(tokens, gubuf[slot, 0])
        up = dot(tokens, gubuf[slot, 1])
        return (gate * jax.nn.sigmoid(gate) * up).astype(BF)

    def three_quarters(b):
        def step(j, c):
            slot = wrap(t + j + j // 2, 4)
            hidden = hidden_units(slot, b)
            for n in range(4):
                cols = slice(n * 512, (n + 1) * 512)
                acc[b, :, cols] += dot(hidden, dnbuf[slot, :, cols])
            return c

        lax.fori_loop(0, 3, step, 0)

    def routes_of(b):
        lanes = lax.broadcasted_iota(jnp.int32, (256, 128), 1)
        parts = xrow[b, :, D:].astype(F32)
        return jnp.sum(jnp.where(lax.rem(lanes, 16) == e, parts, 0.0), axis=1, keepdims=True)

    def last_down(b, c):
        for n in (2 * c, 2 * c + 1):
            cols = slice(n * 512, (n + 1) * 512)
            whole = (acc[b, :, cols] + dot(last_hidden[b], dnbuf[opposite, :, cols])) * route[b]
            for i, o in enumerate((b, 3 - b)):
                for h in (0, 1):
                    at = i * 128 + h * 64
                    obuf[h, wrap(firsts[h] + o, 4), :, :, cols] = (
                        whole[at:at + 64].astype(BF).reshape(4, 16, 512)
                    )

    opposite = wrap(t + 2, 4)
    arrived(far_second[0])
    arrived(far_second[3])
    fill(0)
    arrived(down_across)
    three_quarters(0)
    arrived(up_second)
    up_across = remote(up_view(opposite, None), up_view(opposite, None), partner)
    arrived(far_second[1])
    arrived(far_second[2])
    fill(1)
    three_quarters(1)
    arrived([up_across])
    route = [routes_of(b) for b in (0, 1)]
    for b in (0, 1):
        last_hidden[b] = hidden_units(opposite, b)
    arrived(down_second)
    down_across = remote(down_view(opposite, None), down_view(opposite, None), partner)
    arrived([down_across])

    both = ((0, 1), (1, -1))

    def far_at(h):
        def at(step, cols):
            return obuf.at[h, wrap(firsts[h] + step, 4), ALL, ALL, cols]

        return at

    def near_at(h):
        def at(step, cols):
            return row_sum.at[h, wrap(seconds[h] + step, 4), ALL, cols]

        return at

    def part_of(c, i):
        return pl.ds(c * 1024 + i * 512, 512)

    def send_opposite(at, to, half, h, c):
        return [remote(at(2, part_of(c, i)), half.at[h, c, i], to[h](k)) for i, k in both]

    def send_sides(at, to, half, full, h, c, pending):
        arrived(pending)
        for i, k in both:
            ref = at(k, part_of(c, i))
            ref[...] = (ref[...].astype(F32) + half[h, c, i].astype(F32)).astype(BF)
        whole = pl.ds(c * 1024, 1024)
        return [remote(at(k, whole), full.at[h, c, i], to[h](k)) for i, k in both]

    chains = [(h, c) for c in (0, 1) for h in (0, 1)]
    flight = {}
    for c in (0, 1):
        last_down(1, c)
        for h in (0, 1):
            flight[h, c] = send_opposite(far_at(h), near_to, far_near, h, c)
    for c in (0, 1):
        last_down(0, c)
        for h in (0, 1):
            flight[h, c] = send_sides(
                far_at(h), near_to, far_near, far_sum, h, c, flight[h, c]
            )
    for h, c in chains:
        arrived(flight[h, c])
        whole = pl.ds(c * 1024, 1024)
        total = far_at(h)(0, whole)[...].astype(F32)
        total = total + far_sum[h, c, 0].astype(F32) + far_sum[h, c, 1].astype(F32)
        row_sum[h, :, :, c * 1024:(c + 1) * 1024] = total.astype(BF)
        flight[h, c] = send_opposite(near_at(h), far_to, near_half, h, c)
    for h, c in chains:
        flight[h, c] = send_sides(
            near_at(h), far_to, near_half, near_sum, h, c, flight[h, c]
        )
    def out_copy(src, rows, send, recv, peer):
        return pltpu.make_async_remote_copy(
            src_ref=src, dst_ref=out_ref.at[rows], send_sem=out_sems.at[0, send],
            recv_sem=out_sems.at[1, recv], device_id=peer, device_id_type=MESH,
        )

    for h, c in chains:
        arrived(flight[h, c])
        rows = slice(h * 16, (h + 1) * 16)
        for j in (0, 1):
            cols = slice(c * 1024 + j * 512, c * 1024 + (j + 1) * 512)
            here = slice(j * 512, (j + 1) * 512)
            total = resid[rows, cols] + near_at(h)(0, cols)[...].astype(F32)
            for i in (0, 1):
                total = total + near_sum[h, c, i, :, here].astype(F32)
            fin[2 * c + j, rows] = total.astype(BF)
        if h == 1:
            for j in (2 * c, 2 * c + 1):

                @pl.when(t != j)
                def _(j=j):
                    out_copy(fin.at[j], own_rows, j, t, dev(dp, e, j)).start()

    last = local(fin.at[t], out_ref.at[own_rows])
    last.wait()
    for i, peer in zip(tensor_ids, tensor_peers):
        from_peer = pl.ds(pl.multiple_of(i * 32, 32), 32)
        out_copy(fin.at[i], from_peer, i, i, peer).wait()
    for copy in sent:
        copy.wait_send()


def body(
    hidden_in, queries, new_keys, new_values, prefix_keys, prefix_values, node_length, parent,
    leaf_of_request, out_weight, norm_gain, expert_ids, gate_weights, gate_up, down_weight,
):
    smem = pl.BlockSpec(memory_space=pltpu.SMEM)
    vmem = pl.BlockSpec(memory_space=pltpu.VMEM)
    hbm = pl.BlockSpec(memory_space=pl.ANY)
    return pl.pallas_call(
        kernel,
        out_shape=jax.ShapeDtypeStruct(hidden_in.shape, BF),
        in_specs=[smem] * 3 + [hbm] * 12,
        out_specs=vmem,
        scratch_shapes=[
            pltpu.VMEM((2, 4, 2, 4, 4, 16, 512), BF),
            pltpu.VMEM((4, 4, 512, 128), BF),
            pltpu.VMEM((4, 2, 2048, 256), BF),
            pltpu.VMEM((4, 256, 2048), BF),
            pltpu.VMEM((4, 1, 512), F32),
            pltpu.VMEM((4, 32, 2048), BF),
            pltpu.VMEM((4, 32, 2048), BF),
            pltpu.VMEM((32, 2048), F32),
            pltpu.VMEM((2, 4, 4, 16, 2176), BF),
            pltpu.VMEM((2, 256, 2176), BF),
            pltpu.VMEM((2, 256, 2048), F32),
            pltpu.VMEM((2, 4, 4, 16, 2048), BF),
            pltpu.VMEM((4, 32, 512), BF),
            pltpu.VMEM((128, 512), BF),
            pltpu.VMEM((2, 128, 8), F32),
            pltpu.VMEM((2, 2, 2, 4, 16, 512), BF),
            pltpu.VMEM((2, 2, 2, 4, 16, 1024), BF),
            pltpu.VMEM((2, 2, 2, 16, 512), BF),
            pltpu.VMEM((2, 2, 2, 16, 1024), BF),
            pltpu.VMEM((2, 4, 16, 2048), BF),
            pltpu.VMEM((2, 256, 256), BF),
            pltpu.VMEM((8, 128), jnp.int32),
            pltpu.VMEM((8, 128), F32),
            pltpu.VMEM((128, 512), BF),
            pltpu.VMEM((128, 512), BF),
            pltpu.VMEM((128, 512), BF),
            pltpu.VMEM((128, 512), BF),
            pltpu.SemaphoreType.DMA((224,)),
            pltpu.SemaphoreType.DMA((224,)),
            pltpu.SemaphoreType.DMA((16,)),
            pltpu.SemaphoreType.DMA((2, 4)),
        ],
        compiler_params=pltpu.CompilerParams(
            collective_id=0, has_side_effects=True, vmem_limit_bytes=56 << 20
        ),
        name="layer",
    )(
        leaf_of_request, parent, node_length, expert_ids.T, gate_weights.T, queries, new_keys,
        new_values, hidden_in, norm_gain[None, :], prefix_keys, prefix_values, out_weight, gate_up[0],
        down_weight[0],
    )


def solution(mesh):
    rows = P(("dp", "expert"), "tensor")
    placed = (
        rows, rows, rows, rows,
        P("dp", "tensor"),
        P("dp", "tensor"),
        P(), P(),
        P(("dp", "expert")),
        P("tensor", "expert"),
        P("tensor"),
        P(("dp", "expert"), None),
        P(("dp", "expert"), None),
        P("expert", None, None, "tensor"),
        P("expert", "tensor", None),
    )
    return jax.shard_map(body, mesh=mesh, in_specs=placed, out_specs=rows, check_vma=False)
```

```python
import math

import jax
import jax.numpy as jnp
from jax import lax
from jax.experimental import pallas as pl
from jax.experimental.pallas import tpu as pltpu
from jax.sharding import PartitionSpec as P

MESH = pl.DeviceIdType.MESH
D = 2048
HEAD_DIM = 128
REQ_LEN = 64
NODE_LEN = 64
ALL = slice(None)
BF = jnp.bfloat16
F32 = jnp.float32


def dot(a, b):
    return jnp.dot(a, b, preferred_element_type=F32)


def wrap(v, n):
    return lax.rem(v + 4 * n, n)


def kernel(
    leaf_ref, parent_ref, length_ref,
    ids_in, gate_in, q_in, k_in, v_in, hidden_in, gain_ref,
    pk_ref, pv_ref, w_ref, gu_ref, dn_ref,
    out_ref,
    kvbuf, wbuf, gubuf, dnbuf, gbuf, psend, precv, resid, xbuf, xrow, acc,
    obuf, fin, attn, routes, far_near, far_sum, near_half, near_sum, row_sum, last_hidden,
    ids_ref, gate_ref, q_ref, k_ref, v_ref, hidden_ref,
    send_sems, recv_sems, local_sems, out_sems,
):
    dp = lax.axis_index("dp")
    e = lax.axis_index("expert")
    t = lax.axis_index("tensor")
    zh, core = dp // 2, lax.rem(dp, 2)
    x, y = e // 4, lax.rem(e, 4)
    z = zh * 4 + t

    def dev(dp_, e_, t_):
        return {"dp": dp_, "expert": e_, "tensor": t_}

    def z_neighbour(step):
        zz = wrap(z + step, 16)
        return dev((zz // 4) * 2 + core, e, lax.rem(zz, 4))

    def x_neighbour(step):
        return dev(dp, wrap(x + step, 4) * 4 + y, t)

    def y_neighbour(step):
        return dev(dp, x * 4 + wrap(y + step, 4), t)

    partner = dev(zh * 2 + (1 - core), e, t)
    tensor_ids = [wrap(t + k, 4) for k in (1, 2, 3)]
    tensor_peers = [dev(dp, e, i) for i in tensor_ids]

    def z_hi_neighbour(step):
        return dev(wrap(zh + step, 4) * 2 + core, e, t)

    barrier = pltpu.get_barrier_semaphore()
    greeted = [partner] + tensor_peers
    for to in (x_neighbour, y_neighbour, z_neighbour, z_hi_neighbour):
        greeted += [to(1), to(-1)]
    for peer in greeted:
        pl.semaphore_signal(barrier, inc=1, device_id=peer, device_id_type=MESH)

    counts = [0, 0]
    sent = []

    def local(src, dst):
        copy = pltpu.make_async_copy(src, dst, local_sems.at[counts[1]])
        counts[1] += 1
        copy.start()
        return copy

    def remote(src, dst, peer):
        i = counts[0]
        counts[0] += 1
        copy = pltpu.make_async_remote_copy(
            src_ref=src, dst_ref=dst, send_sem=send_sems.at[i], recv_sem=recv_sems.at[i],
            device_id=peer, device_id_type=MESH,
        )
        copy.start()
        sent.append(copy)
        return copy

    def arrived(copies):
        for copy in copies:
            copy.wait_recv()

    def ag_first(view, phase):
        copies = []
        for h in (0, 1):
            p1, p2 = (x, y) if h == 0 else (y, x)
            to = (x_neighbour, y_neighbour)[(h + phase) % 2]
            own = view(h, p1, p2, None) if phase == 0 else view(h, ALL, p2, None)
            for step in (1, -1):
                copies.append(remote(own, own, to(step)))
        return copies

    def ag_second(view, phase):
        copies = []
        for h in (0, 1):
            p1, p2 = (x, y) if h == 0 else (y, x)
            to = (x_neighbour, y_neighbour)[(h + phase) % 2]
            for sub, step in ((0, 1), (1, -1)):
                if phase == 0:
                    slot = view(h, wrap(p1 - step, 4), p2, sub)
                else:
                    slot = view(h, ALL, wrap(p2 - step, 4), sub)
                copies.append(remote(slot, slot, to(step)))
        return copies

    def w_view(h, a1, a2, sub):
        xi, yi = (a1, a2) if h == 0 else (a2, a1)
        start = core * 256 + h * 128
        rows = pl.ds(start, 128) if sub is None else pl.ds(start + sub * 64, 64)
        return wbuf.at[xi, yi, rows]

    def kv_view(zs):
        def view(h, a1, a2, sub):
            xi, yi = (a1, a2) if h == 0 else (a2, a1)
            cols = ALL if sub is None else pl.ds(sub * 256, 256)
            return kvbuf.at[h, zs, core, xi, yi, ALL, cols]

        return view

    def gather(view, done):
        for phase in (0, 1):
            copies = ag_first(view, phase)
            yield
            arrived(copies)
            copies = ag_second(view, phase)
            yield
            arrived(copies)
        done()
        yield

    rows16 = pl.ds(pl.multiple_of(e * 16, 16), 16)
    w_rows = pl.ds(pl.multiple_of(core * 256, 256), 256)
    own_w = local(w_ref.at[w_rows], wbuf.at[x, y, w_rows])
    own_kv = [
        local(pk_ref.at[rows16], kvbuf.at[0, zh, core, x, y]),
        local(pv_ref.at[rows16], kvbuf.at[1, zh, core, x, y]),
    ]
    own_rows = pl.ds(pl.multiple_of(t * 32, 32), 32)
    own_gain = local(gain_ref, gbuf.at[t])
    own_routes = [local(ids_in, ids_ref), local(gate_in, gate_ref)]
    own_inputs = [
        local(src, dst) for src, dst in (
            (q_in, q_ref), (k_in, k_ref), (v_in, v_ref), (hidden_in, hidden_ref)
        )
    ]
    own_weights = [local(gu_ref, gubuf.at[t]), local(dn_ref, dnbuf.at[t])]

    pl.semaphore_wait(barrier, len(greeted))

    z_copies = []
    for step in (1, -1):
        for i, ref in ((0, pk_ref), (1, pv_ref)):
            z_copies.append(
                remote(ref.at[rows16], kvbuf.at[i, zh, core, x, y], z_hi_neighbour(step))
            )
    for copy in own_kv:
        copy.wait()
    p_partner, w_partner = [], []

    def prefix_gather(zs):
        def done():
            for i in (0, 1):
                piece = kvbuf.at[i, zs, core]
                p_partner.append(remote(piece, piece, partner))

        return gather(kv_view(zs), done)

    def w_done():
        rows = wbuf.at[:, :, w_rows]
        w_partner.append(remote(rows, rows, partner))

    mine, w_all = prefix_gather(zh), gather(w_view, w_done)
    next(mine)
    own_w.wait()
    next(w_all)
    half_rows = pl.ds(pl.multiple_of(core * 128, 128), 128)

    def up_rows(start, size):
        rows = pl.ds(start, size)
        return [
            remote(gu_ref.at[core, rows], gubuf.at[t, core, rows], z_neighbour(k)) for k in (1, -1)
        ]

    up_first = up_rows(0, 256)

    for copy in own_routes:
        copy.wait()
    routes[0] = ids_ref[...].astype(F32).T
    routes[1] = gate_ref[...].T
    named, gates = routes[0, own_rows], routes[1, own_rows]
    lane = lax.broadcasted_iota(jnp.int32, (32, 128), 1)
    lane_expert = jnp.where(lane < 48, lax.rem(lane, 16), -1).astype(F32)
    weight = jnp.zeros((32, 128), F32)
    for i in range(8):
        weight = weight + jnp.where(lane_expert == named[:, i:i + 1], gates[:, i:i + 1], 0.0)
    high = weight.astype(BF)
    rest = weight - high.astype(F32)
    middle = rest.astype(BF)
    low = (rest - middle.astype(F32)).astype(BF)
    routed = jnp.where(lane < 16, high, jnp.where(lane < 32, middle, low))
    firsts, seconds = (x, y), (y, x)
    for h in (0, 1):
        xbuf[h, firsts[h], seconds[h], :, D:] = routed[h * 16:(h + 1) * 16]
    acc[...] = jnp.zeros_like(acc)


    next(mine)
    next(w_all)
    arrived(z_copies)
    z_copies = []
    for i, step in ((0, 1), (1, -1)):
        slot = kvbuf.at[i, wrap(zh - step, 4), core, x, y]
        z_copies.append(remote(slot, slot, z_hi_neighbour(step)))
    up_first += up_rows(256, 1792)

    def down_rows(start):
        rows = pl.ds(pl.multiple_of(core * 128 + start, 64), 64)
        return [remote(dn_ref.at[rows], dnbuf.at[t, rows], z_neighbour(k)) for k in (1, -1)]

    down_first = down_rows(0)
    small_copies = [remote(gain_ref, gbuf.at[t], peer) for peer in tensor_peers]
    before, behind = prefix_gather(wrap(zh - 1, 4)), prefix_gather(wrap(zh + 1, 4))
    next(before)
    next(behind)
    next(mine)
    next(w_all)
    next(before)
    next(behind)
    next(mine)
    arrived(z_copies)
    across = prefix_gather(wrap(zh + 2, 4))
    next(across)
    next(w_all)
    next(before)
    next(behind)
    next(mine)
    next(across)
    next(before)
    next(behind)
    next(w_all)
    next(across)
    next(before)
    next(behind)
    next(across)
    next(across)

    def pass_on(arrivals, views):
        arrived(arrivals)
        on, across = [], []
        for sub, step in ((0, 1), (1, -1)):
            slot = wrap(t - step, 4)
            part = views(slot, sub)
            on.append(remote(part, part, z_neighbour(step)))
            whole = views(slot, None)
            across.append(remote(whole, whole, partner))
        return on, across

    def up_view(slot, sub):
        return gubuf.at[slot, core, ALL if sub is None else pl.ds(sub * 1024, 1024)]

    def down_view(slot, sub):
        return dnbuf.at[slot, half_rows, ALL if sub is None else pl.ds(sub * 1024, 1024)]

    for copy in own_inputs:
        copy.wait()
    arrived(p_partner)

    row_id = lax.broadcasted_iota(jnp.int32, (REQ_LEN, 256), 0)
    col_id = lax.broadcasted_iota(jnp.int32, (REQ_LEN, 256), 1)
    in_node = lax.rem(col_id, NODE_LEN)
    piece = col_id // NODE_LEN
    for r in range(2):
        leaf = leaf_ref[r]
        tenant = parent_ref[leaf]
        root = parent_ref[tenant]
        nodes = (leaf, tenant, root)
        limit = jnp.where(
            piece == 0, length_ref[leaf],
            jnp.where(piece == 1, length_ref[tenant],
                      jnp.where(piece == 2, length_ref[root], row_id + 1)),
        )
        allowed = in_node < limit

        def rows_of(i, own):
            parts = [
                kvbuf[i, n // 8, lax.rem(n // 4, 2), lax.rem(n, 4)].reshape(NODE_LEN, 512)
                for n in nodes
            ]
            return jnp.concatenate(parts + [own[r * REQ_LEN:(r + 1) * REQ_LEN]], axis=0)

        keys = rows_of(0, k_ref)
        values = rows_of(1, v_ref)
        for h in range(4):
            cols = slice(h * HEAD_DIM, (h + 1) * HEAD_DIM)
            qh = q_ref[r * REQ_LEN:(r + 1) * REQ_LEN, cols]
            scores = lax.dot_general(
                qh, keys[:, cols], (((1,), (1,)), ((), ())), preferred_element_type=F32
            ) * (1.0 / math.sqrt(HEAD_DIM))
            top = jnp.max(jnp.where(allowed, scores, -1e30), axis=-1, keepdims=True)
            weights = jnp.where(allowed, jnp.exp(scores - top), 0.0)
            total = jnp.sum(weights, axis=-1, keepdims=True)
            summed = dot(weights.astype(BF), values[:, cols])
            attn[r * REQ_LEN:(r + 1) * REQ_LEN, cols] = (summed / total).astype(BF)

    arrived(w_partner)
    for i in range(16):
        part = dot(attn[...], wbuf[i // 4, i % 4])
        mine_too = (t == i // 4).astype(F32)
        part = part + mine_too * hidden_ref[:, (i % 4) * 128:(i % 4 + 1) * 128].astype(F32)
        psend[:, :, i * 128:(i + 1) * 128] = part.astype(BF).reshape(4, 32, 128)
    base = counts[0]
    counts[0] += 3

    def proj_copy(k):
        i = wrap(t + k, 4)
        return pltpu.make_async_remote_copy(
            src_ref=psend.at[i], dst_ref=precv.at[t], send_sem=send_sems.at[base + k - 1],
            recv_sem=recv_sems.at[base + k - 1], device_id=dev(dp, e, i), device_id_type=MESH,
        )

    edge_first = jnp.where(t == 0, 3, jnp.where(t == 3, 1, 2))
    edge_second = jnp.where(t == 0, 2, jnp.where(t == 1, 1, jnp.where(t == 2, 3, 2)))
    for k in (edge_first, edge_second, 6 - edge_first - edge_second):
        proj_copy(k).start()
    proj_copies = [proj_copy(k) for k in (1, 2, 3)]
    sent.extend(proj_copies)
    down_first += down_rows(64)
    own_gain.wait()
    arrived(small_copies)
    arrived(proj_copies)
    up_second, up_across = pass_on(up_first, up_view)

    square = jnp.zeros((32, 1), F32)
    for j in range(4):
        cols = slice(j * 512, (j + 1) * 512)
        total = psend[t, :, cols].astype(F32)
        for i in tensor_ids:
            total = total + precv[i, :, cols].astype(F32)
        resid[:, cols] = total
        square = square + jnp.sum(total * total, axis=1, keepdims=True)
    factor = lax.rsqrt(square / D + 1e-05)
    for j in range(4):
        cols = slice(j * 512, (j + 1) * 512)
        normed = (resid[:, cols] * factor * gbuf[j]).astype(BF)
        for h in (0, 1):
            xbuf[h, firsts[h], seconds[h], :, cols] = normed[h * 16:(h + 1) * 16]

    near_to, far_to = (x_neighbour, y_neighbour), (y_neighbour, x_neighbour)
    col_parts = (pl.ds(0, 1152), pl.ds(1152, 1024))

    def spread(o1, o2, to):
        copies = []
        for h in (0, 1):
            slot = xbuf.at[h, wrap(firsts[h] + o1, 4), wrap(seconds[h] + o2, 4)]
            copies += [remote(slot, slot, to[h](step)) for step in (1, -1)]
        return copies

    def relay(near, o1, o2, to):
        copies = []
        for sub, step in ((0, 1), (1, -1)):
            for h in (0, 1):
                a1 = wrap(firsts[h] + (-step if near else o1), 4)
                a2 = wrap(seconds[h] + (o2 if near else -step), 4)
                slot = xbuf.at[h, a1, a2, ALL, col_parts[sub]]
                copies.append(remote(slot, slot, to[h](step)))
        return copies

    near_first = spread(0, 0, near_to)
    far_first = {0: spread(0, 0, far_to)}
    far_second = {}
    arrived(near_first)
    near_second = relay(True, None, 0, near_to)
    far_first[3] = spread(-1, 0, far_to)
    far_first[1] = spread(1, 0, far_to)
    arrived(far_first[0])
    far_second[0] = relay(False, 0, None, far_to)
    arrived(near_second)
    far_first[2] = spread(2, 0, far_to)
    down_second, down_across = pass_on(down_first, down_view)
    arrived(far_first[3])
    far_second[3] = relay(False, 3, None, far_to)
    arrived(far_first[1])
    far_second[1] = relay(False, 1, None, far_to)
    arrived(far_first[2])
    far_second[2] = relay(False, 2, None, far_to)
    for copy in own_weights:
        copy.wait()
    arrived(up_across)

    def fill(b):
        for i, o in enumerate((b, 3 - b)):
            for h in (0, 1):
                at = i * 128 + h * 64
                rows = xbuf[h, wrap(firsts[h] + o, 4)]
                xrow[b, at:at + 64] = rows.reshape(64, D + 128)

    def hidden_units(slot, b):
        tokens = xrow[b, :, 0:D]
        gate = dot(tokens, gubuf[slot, 0])
        up = dot(tokens, gubuf[slot, 1])
        return (gate * jax.nn.sigmoid(gate) * up).astype(BF)

    def three_quarters(b):
        def step(j, c):
            slot = wrap(t + j + j // 2, 4)
            hidden = hidden_units(slot, b)
            for n in range(4):
                cols = slice(n * 512, (n + 1) * 512)
                acc[b, :, cols] += dot(hidden, dnbuf[slot, :, cols])
            return c

        lax.fori_loop(0, 3, step, 0)

    def routes_of(b):
        lanes = lax.broadcasted_iota(jnp.int32, (256, 128), 1)
        parts = xrow[b, :, D:].astype(F32)
        return jnp.sum(jnp.where(lax.rem(lanes, 16) == e, parts, 0.0), axis=1, keepdims=True)

    def last_down(b, c):
        for n in (2 * c, 2 * c + 1):
            cols = slice(n * 512, (n + 1) * 512)
            whole = (acc[b, :, cols] + dot(last_hidden[b], dnbuf[opposite, :, cols])) * route[b]
            for i, o in enumerate((b, 3 - b)):
                for h in (0, 1):
                    at = i * 128 + h * 64
                    obuf[h, wrap(firsts[h] + o, 4), :, :, cols] = (
                        whole[at:at + 64].astype(BF).reshape(4, 16, 512)
                    )

    opposite = wrap(t + 2, 4)
    arrived(far_second[0])
    arrived(far_second[3])
    fill(0)
    arrived(down_across)
    three_quarters(0)
    arrived(up_second)
    up_across = remote(up_view(opposite, None), up_view(opposite, None), partner)
    arrived(far_second[1])
    arrived(far_second[2])
    fill(1)
    three_quarters(1)
    arrived([up_across])
    route = [routes_of(b) for b in (0, 1)]
    for b in (0, 1):
        last_hidden[b] = hidden_units(opposite, b)
    arrived(down_second)
    down_across = remote(down_view(opposite, None), down_view(opposite, None), partner)
    arrived([down_across])

    both = ((0, 1), (1, -1))

    def far_at(h):
        def at(step, cols):
            return obuf.at[h, wrap(firsts[h] + step, 4), ALL, ALL, cols]

        return at

    def near_at(h):
        def at(step, cols):
            return row_sum.at[h, wrap(seconds[h] + step, 4), ALL, cols]

        return at

    def part_of(c, i):
        return pl.ds(c * 1024 + i * 512, 512)

    def send_opposite(at, to, half, h, c):
        return [remote(at(2, part_of(c, i)), half.at[h, c, i], to[h](k)) for i, k in both]

    def send_sides(at, to, half, full, h, c, pending):
        arrived(pending)
        for i, k in both:
            ref = at(k, part_of(c, i))
            ref[...] = (ref[...].astype(F32) + half[h, c, i].astype(F32)).astype(BF)
        whole = pl.ds(c * 1024, 1024)
        return [remote(at(k, whole), full.at[h, c, i], to[h](k)) for i, k in both]

    chains = [(h, c) for c in (0, 1) for h in (0, 1)]
    flight = {}
    for c in (0, 1):
        last_down(1, c)
        for h in (0, 1):
            flight[h, c] = send_opposite(far_at(h), near_to, far_near, h, c)
    for c in (0, 1):
        last_down(0, c)
        for h in (0, 1):
            flight[h, c] = send_sides(
                far_at(h), near_to, far_near, far_sum, h, c, flight[h, c]
            )
    for h, c in chains:
        arrived(flight[h, c])
        whole = pl.ds(c * 1024, 1024)
        total = far_at(h)(0, whole)[...].astype(F32)
        total = total + far_sum[h, c, 0].astype(F32) + far_sum[h, c, 1].astype(F32)
        row_sum[h, :, :, c * 1024:(c + 1) * 1024] = total.astype(BF)
        flight[h, c] = send_opposite(near_at(h), far_to, near_half, h, c)
    for h, c in chains:
        flight[h, c] = send_sides(
            near_at(h), far_to, near_half, near_sum, h, c, flight[h, c]
        )
    def out_copy(src, rows, send, recv, peer):
        return pltpu.make_async_remote_copy(
            src_ref=src, dst_ref=out_ref.at[rows], send_sem=out_sems.at[0, send],
            recv_sem=out_sems.at[1, recv], device_id=peer, device_id_type=MESH,
        )

    for h, c in chains:
        arrived(flight[h, c])
        rows = slice(h * 16, (h + 1) * 16)
        for j in (0, 1):
            cols = slice(c * 1024 + j * 512, c * 1024 + (j + 1) * 512)
            here = slice(j * 512, (j + 1) * 512)
            total = resid[rows, cols] + near_at(h)(0, cols)[...].astype(F32)
            for i in (0, 1):
                total = total + near_sum[h, c, i, :, here].astype(F32)
            fin[2 * c + j, rows] = total.astype(BF)
        if h == 1:
            for j in (2 * c, 2 * c + 1):

                @pl.when(t != j)
                def _(j=j):
                    out_copy(fin.at[j], own_rows, j, t, dev(dp, e, j)).start()

    last = local(fin.at[t], out_ref.at[own_rows])
    last.wait()
    for i, peer in zip(tensor_ids, tensor_peers):
        from_peer = pl.ds(pl.multiple_of(i * 32, 32), 32)
        out_copy(fin.at[i], from_peer, i, i, peer).wait()
    for copy in sent:
        copy.wait_send()


def body(
    hidden_in, queries, new_keys, new_values, prefix_keys, prefix_values, node_length, parent,
    leaf_of_request, out_weight, norm_gain, expert_ids, gate_weights, gate_up, down_weight,
):
    smem = pl.BlockSpec(memory_space=pltpu.SMEM)
    vmem = pl.BlockSpec(memory_space=pltpu.VMEM)
    hbm = pl.BlockSpec(memory_space=pl.ANY)
    return pl.pallas_call(
        kernel,
        out_shape=jax.ShapeDtypeStruct(hidden_in.shape, BF),
        in_specs=[smem] * 3 + [hbm] * 12,
        out_specs=vmem,
        scratch_shapes=[
            pltpu.VMEM((2, 4, 2, 4, 4, 16, 512), BF),
            pltpu.VMEM((4, 4, 512, 128), BF),
            pltpu.VMEM((4, 2, 2048, 256), BF),
            pltpu.VMEM((4, 256, 2048), BF),
            pltpu.VMEM((4, 1, 512), F32),
            pltpu.VMEM((4, 32, 2048), BF),
            pltpu.VMEM((4, 32, 2048), BF),
            pltpu.VMEM((32, 2048), F32),
            pltpu.VMEM((2, 4, 4, 16, 2176), BF),
            pltpu.VMEM((2, 256, 2176), BF),
            pltpu.VMEM((2, 256, 2048), F32),
            pltpu.VMEM((2, 4, 4, 16, 2048), BF),
            pltpu.VMEM((4, 32, 512), BF),
            pltpu.VMEM((128, 512), BF),
            pltpu.VMEM((2, 128, 8), F32),
            pltpu.VMEM((2, 2, 2, 4, 16, 512), BF),
            pltpu.VMEM((2, 2, 2, 4, 16, 1024), BF),
            pltpu.VMEM((2, 2, 2, 16, 512), BF),
            pltpu.VMEM((2, 2, 2, 16, 1024), BF),
            pltpu.VMEM((2, 4, 16, 2048), BF),
            pltpu.VMEM((2, 256, 256), BF),
            pltpu.VMEM((8, 128), jnp.int32),
            pltpu.VMEM((8, 128), F32),
            pltpu.VMEM((128, 512), BF),
            pltpu.VMEM((128, 512), BF),
            pltpu.VMEM((128, 512), BF),
            pltpu.VMEM((128, 512), BF),
            pltpu.SemaphoreType.DMA((224,)),
            pltpu.SemaphoreType.DMA((224,)),
            pltpu.SemaphoreType.DMA((16,)),
            pltpu.SemaphoreType.DMA((2, 4)),
        ],
        compiler_params=pltpu.CompilerParams(
            collective_id=0, has_side_effects=True, vmem_limit_bytes=56 << 20
        ),
        name="layer",
    )(
        leaf_of_request, parent, node_length, expert_ids.T, gate_weights.T, queries, new_keys,
        new_values, hidden_in, norm_gain[None, :], prefix_keys, prefix_values, out_weight, gate_up[0],
        down_weight[0],
    )


def solution(mesh):
    rows = P(("dp", "expert"), "tensor")
    placed = (
        rows, rows, rows, rows,
        P("dp", "tensor"),
        P("dp", "tensor"),
        P(), P(),
        P(("dp", "expert")),
        P("tensor", "expert"),
        P("tensor"),
        P(("dp", "expert"), None),
        P(("dp", "expert"), None),
        P("expert", None, None, "tensor"),
        P("expert", "tensor", None),
    )
    return jax.shard_map(body, mesh=mesh, in_specs=placed, out_specs=rows, check_vma=False)
```
